256 devices in a mesh: seq: 64 (over x, z, core), head: 4 (over y).
Axes of the slice: x: 4, y: 4, z: 8, core: 2. Of those that a mesh axis runs over, the one named last changes fastest.
Arguments:
- query_rows: bfloat16 [1, 16384, 2048], P(None, 'seq', 'head'), may hold values from -28 to 28
- key_rows: bfloat16 [1, 16384, 2048], P(None, 'seq', 'head'), may hold values from -4 to 4
- value_rows: bfloat16 [1, 16384, 2048], P(None, 'seq', 'head'), may hold values from -6 to 6
- grad_out: bfloat16 [1, 16384, 2048], P(None, 'seq', 'head'), may hold values from -6 to 6
- rand_blocks: int32 [1, 16, 256, 3], P(None, 'head'), may hold values from 0 to 255, as said below
- global_pos: int32 [128], replicated, may hold values from 0 to 16383, as said below
Outputs:
- attended: bfloat16 [1, 16384, 2048], P(None, 'seq', 'head')
- grad_query: bfloat16 [1, 16384, 2048], P(None, 'seq', 'head')
- grad_key: bfloat16 [1, 16384, 2048], P(None, 'seq', 'head')
- grad_value: bfloat16 [1, 16384, 2048], P(None, 'seq', 'head')
The draws below stay inside these ranges and needn't reach their ends.
Inputs may be any that keep to these rules, and one draw needn't show every extreme that they name: `rand_blocks`: for each run of 4 query blocks and each run of 4 heads that start at multiples of these counts, taking the one sequence and all 3 picks together, at most 1 picks name a block of any one run of 4 key blocks that starts at a multiple of 4; in each such run of query blocks and heads some run of key blocks is named exactly 1 times. `global_pos`: distinct positions; the first and the last token of the sequence are among them.
All inputs are finite; a program needn't handle non-finite values.
Results may differ from the reference program's by a relative error of at most 0.006.
The reference program's roundings to bfloat16 on the way (of `weights_b` and `dscore_b`) count: a program that leaves them out, or rounds other values in their place, can miss the bound.
Values may be sent and summed in bfloat16 or wider, within the bound.
A program may use at most 64 MiB of HBM per device.

```python
from functools import partial
import jax
import jax.numpy as jnp
from jax import lax

HEADS = 16
HEAD_DIM = 128
BLOCK = 64
RAND = 3
GLOBALS = 128
BATCH = 1
BLK_DEV = 4
HEAD_DEV = 4
NBLOCKS = 256
SEQ = 16384
NKEYS = 512


def attention_pair(key):
    base_key = jax.random.fold_in(key, 11)
    first_key, second_key = jax.random.split(base_key, 2)
    dims_all = (BATCH, SEQ, HEADS, HEAD_DIM)
    query_part = jnp.clip(jax.random.normal(first_key, dims_all, jnp.float32), -4.0, 4.0)
    key_part = jnp.clip(jax.random.normal(second_key, dims_all, jnp.float32), -4.0, 4.0)
    return (query_part.reshape(BATCH, SEQ, HEADS * HEAD_DIM), key_part.reshape(BATCH, SEQ, HEADS * HEAD_DIM))


def draw_query_rows(key, part):
    return attention_pair(key)[0].astype(jnp.bfloat16)


def draw_key_rows(key, part):
    return attention_pair(key)[1].astype(jnp.bfloat16)


def draw_rand_blocks(key, part):
    groups = NBLOCKS // BLK_DEV
    head_groups = HEADS // HEAD_DEV
    slot_count = BATCH * HEAD_DEV * BLK_DEV * RAND
    most = (slot_count + groups - 1) // groups

    def one_group(group_key):
        hold_key, place_key = jax.random.split(group_key)
        holders = jax.random.permutation(hold_key, jnp.arange(groups * most, dtype=jnp.int32) % groups)[:slot_count]
        local_block = jax.random.randint(place_key, (slot_count,), 0, BLK_DEV, dtype=jnp.int32)
        return holders * BLK_DEV + local_block
    table = jax.vmap(one_group)(jax.random.split(key, groups * head_groups))
    table = table.reshape(groups, head_groups, BATCH, HEAD_DEV, BLK_DEV, RAND).transpose(2, 1, 3, 0, 4, 5)
    return table.reshape(BATCH, HEADS, NBLOCKS, RAND).astype(jnp.int32)


def draw_global_pos(key, part):
    middle = jax.random.permutation(key, SEQ - 2)[:GLOBALS - 2].astype(jnp.int32) + 1
    return jnp.concatenate([jnp.zeros((1,), jnp.int32), middle, jnp.full((1,), SEQ - 1, jnp.int32)])


def block_scale(own_key, extent, cuts, smallest, high):
    level = 1.0
    for axis_at, parts in cuts:
        heights = jax.random.uniform(jax.random.fold_in(jax.random.fold_in(own_key, 6), axis_at), (parts,), jnp.float32, smallest / len(cuts), high / len(cuts))
        level = level * jnp.repeat(jnp.exp(heights), extent[axis_at] // parts).reshape((-1,) + (1,) * (len(extent) - 1 - axis_at))
    return level


def centred(own_key, dims, scale, most, shards=(), kind=jnp.bfloat16):
    factor_of = block_scale(own_key, dims, shards, -0.22, 0.18) if shards else 1.0
    result = jax.random.normal(own_key, dims, jnp.float32) * scale * factor_of
    return jnp.minimum(jnp.maximum(result, -most), most).astype(kind)


def setup_inputs(seed: int = 0) -> dict:
    streams_of = jax.random.split(jax.random.key(seed), 7)
    query_rows = draw_query_rows(jax.random.fold_in(streams_of[6], 71), 0)
    key_rows = draw_key_rows(jax.random.fold_in(streams_of[6], 71), 0)
    value_rows = centred(streams_of[2], (BATCH, SEQ, HEADS * HEAD_DIM), 1.0, 6.0, ((1, 64), (2, 4)))
    grad_out = centred(streams_of[3], (BATCH, SEQ, HEADS * HEAD_DIM), 1.0, 6.0, ((1, 64), (2, 4)))
    rand_blocks = draw_rand_blocks(jax.random.fold_in(streams_of[6], 71), 0)
    global_pos = draw_global_pos(jax.random.fold_in(streams_of[6], 71), 0)
    return {"query_rows": query_rows, "key_rows": key_rows, "value_rows": value_rows, "grad_out": grad_out, "rand_blocks": rand_blocks, "global_pos": global_pos}


def rounded(values):
    return lax.optimization_barrier(values.astype(jnp.bfloat16)).astype(jnp.float32)


def one_head(operands, global_pos):
    query_one, key_one, value_one, grad_one, table_one = operands
    score_scale = HEAD_DIM ** -0.5
    query_blocks = query_one.astype(jnp.float32).reshape(NBLOCKS, BLOCK, HEAD_DIM)
    grad_blocks = grad_one.astype(jnp.float32).reshape(NBLOCKS, BLOCK, HEAD_DIM)

    def key_list(token_rows):
        token_rows = token_rows.astype(jnp.float32)
        blocks = token_rows.reshape(NBLOCKS, BLOCK, HEAD_DIM)
        empty = jnp.zeros((1, BLOCK, HEAD_DIM), jnp.float32)
        padded = jnp.concatenate([empty, blocks, empty], axis=0)
        window_part = jnp.concatenate([padded[:-2], padded[1:-1], padded[2:]], axis=1)
        random_part = blocks[table_one].reshape(NBLOCKS, RAND * BLOCK, HEAD_DIM)
        global_part = jnp.broadcast_to(token_rows[global_pos][None], (NBLOCKS, GLOBALS, HEAD_DIM))
        return jnp.concatenate([window_part, random_part, global_part], axis=1)

    key_lists = key_list(key_one)
    value_lists = key_list(value_one)
    block_ids = jnp.arange(NBLOCKS)
    column_ids = jnp.arange(NKEYS)[None, :]
    middle_ok = jnp.where((column_ids >= 2 * BLOCK) & (column_ids < 3 * BLOCK), (block_ids < NBLOCKS - 1)[:, None], True)
    valid_mask = jnp.where(column_ids < BLOCK, (block_ids > 0)[:, None], middle_ok)
    scores = jnp.einsum('jqd,jkd->jqk', query_blocks, key_lists) * score_scale
    scores = jnp.where(valid_mask[:, None, :], scores, -1e30)
    row_max = jnp.max(scores, axis=-1, keepdims=True)
    log_total = row_max + jnp.log(jnp.sum(jnp.exp(scores - row_max), axis=-1, keepdims=True))
    weights = jnp.exp(scores - log_total)
    weights_b = rounded(weights)
    mixed_rows = jnp.einsum('jqk,jkd->jqd', weights_b, value_lists)
    row_delta = jnp.sum(grad_blocks * mixed_rows, axis=-1, keepdims=True)
    grad_probs = jnp.einsum('jqd,jkd->jqk', grad_blocks, value_lists)
    dscore_b = rounded(weights * (grad_probs - row_delta))
    grad_query = jnp.einsum('jqk,jkd->jqd', dscore_b, key_lists) * score_scale
    key_terms = jnp.einsum('jqk,jqd->jkd', dscore_b, query_blocks) * score_scale
    value_terms = jnp.einsum('jqk,jqd->jkd', weights_b, grad_blocks)

    def collect(terms):
        window_terms = terms[:, :3 * BLOCK].reshape(NBLOCKS, 3, BLOCK, HEAD_DIM)
        padded = jnp.zeros((NBLOCKS + 2, BLOCK, HEAD_DIM), jnp.float32)
        padded = padded.at[0:NBLOCKS].add(window_terms[:, 0])
        padded = padded.at[1:NBLOCKS + 1].add(window_terms[:, 1])
        padded = padded.at[2:NBLOCKS + 2].add(window_terms[:, 2])
        blocks = padded[1:-1]
        random_terms = terms[:, 3 * BLOCK:(3 + RAND) * BLOCK].reshape(NBLOCKS, RAND, BLOCK, HEAD_DIM)
        blocks = blocks.at[table_one].add(random_terms)
        token_rows = blocks.reshape(SEQ, HEAD_DIM)
        return token_rows.at[global_pos].add(jnp.sum(terms[:, (3 + RAND) * BLOCK:], axis=0))

    return (mixed_rows.reshape(SEQ, HEAD_DIM).astype(jnp.bfloat16),
            grad_query.reshape(SEQ, HEAD_DIM).astype(jnp.bfloat16),
            collect(key_terms).astype(jnp.bfloat16),
            collect(value_terms).astype(jnp.bfloat16))


def heads_first(array):
    return array.reshape(BATCH, SEQ, HEADS, HEAD_DIM).transpose(0, 2, 1, 3).reshape(BATCH * HEADS, SEQ, HEAD_DIM)


def heads_back(array):
    return array.reshape(BATCH, HEADS, SEQ, HEAD_DIM).transpose(0, 2, 1, 3).reshape(BATCH, SEQ, HEADS * HEAD_DIM)


def reference(query_rows, key_rows, value_rows, grad_out, rand_blocks, global_pos):
    operands = (heads_first(query_rows), heads_first(key_rows), heads_first(value_rows),
                heads_first(grad_out), rand_blocks.reshape(BATCH * HEADS, NBLOCKS, RAND))
    results = lax.map(partial(one_head, global_pos=global_pos), operands)
    return (heads_back(results[0]), heads_back(results[1]), heads_back(results[2]), heads_back(results[3]))
```

```python
import functools

import jax
import jax.numpy as jnp
from jax import lax
from jax.experimental import pallas as pl
from jax.experimental.pallas import tpu as pltpu
from jax.sharding import PartitionSpec as P

BLOCK = 64
DIM = 128
HEADS = 4
BLOCKS = 4
PICKS = 3
TOK = BLOCK * BLOCKS
COLS = HEADS * DIM
GLOB = 128
TILE = 16
GROUPS = GLOB // TILE
BF16 = jnp.bfloat16
F32 = jnp.float32
MESH = pl.DeviceIdType.MESH
VMEM = pl.BlockSpec(memory_space=pltpu.VMEM)
SMEM = pl.BlockSpec(memory_space=pltpu.SMEM)


def send_to(peer, src, dst, sems):
    return pltpu.make_async_remote_copy(
        src_ref=src,
        dst_ref=dst,
        send_sem=sems[0],
        recv_sem=sems[1],
        device_id={"seq": peer},
        device_id_type=MESH,
    )


def greet(me, size):
    barrier = pltpu.get_barrier_semaphore()

    @pl.loop(1, size)
    def _(k):
        pl.semaphore_signal(
            barrier,
            inc=1,
            device_id={"seq": lax.rem(me + k, size)},
            device_id_type=MESH,
        )

    return barrier


def exchange(me, size, barrier, edges, edge_out, tiles, part, tile, tiles_out, slots, slots_out, sems):
    edge_sems, part_sems, tile_sems, slot_sems = sems
    right, left = lax.rem(me + 1, size), lax.rem(me + size - 1, size)
    part[me] = tiles[me]
    slots_out[me] = slots[me]
    pl.semaphore_wait(barrier, size - 1)
    copies = [send_to(left, src, edge_out.at[1, at], edge_sems[i]) for i, (src, at) in enumerate(edges[0])]
    copies += [send_to(right, src, edge_out.at[0, at], edge_sems[2 + i]) for i, (src, at) in enumerate(edges[1])]
    for copy in copies:
        copy.start()

    @pl.loop(1, size)
    def _(k):
        peer = lax.rem(me + k, size)
        send_to(peer, tiles.at[peer], part.at[me], part_sems).start()

    @pl.loop(1, size)
    def _(k):
        peer = lax.rem(me + k, size)
        send_to(peer, slots.at[peer], slots_out.at[me], slot_sems).start()

    rest = pl.ds(0, size - 1)
    send_to(right, tiles.at[rest], part.at[rest], part_sems).wait()
    tile[...] = jnp.sum(part[...].astype(F32), axis=0).astype(BF16)
    tiles_out[me] = tile[...]

    @pl.loop(1, size)
    def _(k):
        peer = lax.rem(me + k, size)
        send_to(peer, tile, tiles_out.at[me], tile_sems).start()

    send_to(right, tiles.at[rest], tiles_out.at[rest], tile_sems).wait()
    for copy in copies:
        copy.wait()
    send_to(right, slots.at[rest], slots_out.at[rest], slot_sems).wait()


def sem_pairs(edge, part, tile, slot):
    edge_sems = [(edge.at[0, i], edge.at[1, i]) for i in range(4)]
    return edge_sems, (part.at[0], part.at[1]), (tile.at[0], tile.at[1]), (slot.at[0], slot.at[1])


def fetch_kernel(
    size, want, pos, key, value, slots_out, edge_out, tiles_out, stacked, slots, tiles, part, tile, *dma
):
    me = lax.axis_index("seq")
    barrier = greet(me, size)
    for j in range(BLOCKS):
        for h in range(HEADS):
            rows, cols = pl.ds(j * BLOCK, BLOCK), pl.ds(h * DIM, DIM)
            stacked[j * HEADS + h, :BLOCK] = key[rows, cols]
            stacked[j * HEADS + h, BLOCK:] = value[rows, cols]
    hot = (pos[...] - me * TOK == lax.broadcasted_iota(jnp.int32, (GLOB, TOK), 1)).astype(F32).astype(BF16)
    for c, ref in enumerate((key, value)):
        owned = jnp.dot(hot, ref[...], preferred_element_type=F32).astype(BF16)
        for g in range(GROUPS):
            for h in range(HEADS):
                tiles[g * 2 * HEADS + c * HEADS + h] = owned[g * TILE : (g + 1) * TILE, h * DIM : (h + 1) * DIM]

    @pl.loop(0, size)
    def _(k):
        slots[k] = stacked[want[k]]

    last, first = pl.ds(TOK - BLOCK, BLOCK), pl.ds(0, BLOCK)
    upper, lower = pl.ds(0, BLOCK), pl.ds(BLOCK, BLOCK)
    edges = (
        ((key.at[first], upper), (value.at[first], lower)),
        ((key.at[last], upper), (value.at[last], lower)),
    )
    exchange(me, size, barrier, edges, edge_out, tiles, part, tile, tiles_out, slots, slots_out, sem_pairs(*dma))


def return_kernel(size, edge_in, tiles, slots, edge_out, tiles_out, slots_out, part, tile, *dma):
    me = lax.axis_index("seq")
    barrier = greet(me, size)
    upper, lower = pl.ds(0, BLOCK), pl.ds(BLOCK, BLOCK)
    edges = (
        ((edge_in.at[0, upper], upper), (edge_in.at[0, lower], lower)),
        ((edge_in.at[1, upper], upper), (edge_in.at[1, lower], lower)),
    )
    exchange(me, size, barrier, edges, edge_out, tiles, part, tile, tiles_out, slots, slots_out, sem_pairs(*dma))


def dot_nt(a, b):
    return lax.dot_general(a, b, (((1,), (1,)), ((), ())), preferred_element_type=F32)


def dot_tn(a, b):
    return lax.dot_general(a, b, (((0,), (0,)), ((), ())), preferred_element_type=F32)


def dot_nn(a, b):
    return jnp.dot(a, b, preferred_element_type=F32)


def attention_kernel(
    last_device, table, query, key, value, grad, edge, tiles, slots, attended, grad_query, own_key, own_value, edge_out, tiles_out, slots_out
):
    me = table[HEADS * BLOCKS * PICKS]
    scale = DIM**-0.5
    wide = (BLOCKS + 2) * BLOCK
    query_block = lax.broadcasted_iota(jnp.int32, (TOK, wide), 0) // BLOCK
    key_block = lax.broadcasted_iota(jnp.int32, (TOK, wide), 1) // BLOCK
    low = jnp.where(me == 0, 1, 0)
    high = jnp.where(me == last_device, BLOCKS, BLOCKS + 1)
    offset = key_block - query_block
    band = (offset >= 0) & (offset <= 2) & (key_block >= low) & (key_block <= high)
    for h in range(HEADS):
        cols = pl.ds(h * DIM, DIM)
        q, g = query[:, cols], grad[:, cols]
        keys = jnp.concatenate([edge[0, :BLOCK, cols], key[:, cols], edge[1, :BLOCK, cols]], axis=0)
        values = jnp.concatenate([edge[0, BLOCK:, cols], value[:, cols], edge[1, BLOCK:, cols]], axis=0)
        global_keys = jnp.concatenate([tiles[i * 2 * HEADS + h] for i in range(GROUPS)], axis=0)
        global_values = jnp.concatenate([tiles[i * 2 * HEADS + HEADS + h] for i in range(GROUPS)], axis=0)
        at = lambda j, p: (h * BLOCKS + j) * PICKS + p
        picked_keys = [
            jnp.concatenate([slots[table[at(j, p)], :BLOCK] for p in range(PICKS)], axis=0) for j in range(BLOCKS)
        ]
        picked_values = [
            jnp.concatenate([slots[table[at(j, p)], BLOCK:] for p in range(PICKS)], axis=0) for j in range(BLOCKS)
        ]
        rows = [slice(j * BLOCK, (j + 1) * BLOCK) for j in range(BLOCKS)]
        near = jnp.where(band, dot_nt(q, keys) * scale, -1e30)
        far = jnp.concatenate([dot_nt(q[rows[j]], picked_keys[j]) for j in range(BLOCKS)], axis=0) * scale
        glob = dot_nt(q, global_keys) * scale
        row_max = jnp.maximum(
            jnp.max(near, axis=1, keepdims=True),
            jnp.maximum(jnp.max(far, axis=1, keepdims=True), jnp.max(glob, axis=1, keepdims=True)),
        )
        near, far, glob = jnp.exp(near - row_max), jnp.exp(far - row_max), jnp.exp(glob - row_max)
        total = (
            jnp.sum(near, axis=1, keepdims=True)
            + jnp.sum(far, axis=1, keepdims=True)
            + jnp.sum(glob, axis=1, keepdims=True)
        )
        inverse = 1.0 / total
        near, far, glob = near * inverse, far * inverse, glob * inverse
        near_b, far_b, glob_b = near.astype(BF16), far.astype(BF16), glob.astype(BF16)
        mixed = dot_nn(near_b, values) + dot_nn(glob_b, global_values)
        mixed += jnp.concatenate([dot_nn(far_b[rows[j]], picked_values[j]) for j in range(BLOCKS)], axis=0)
        attended[:, cols] = mixed.astype(BF16)
        delta = jnp.sum(g.astype(F32) * mixed, axis=1, keepdims=True)
        near_d = (near * (dot_nt(g, values) - delta)).astype(BF16)
        glob_d = (glob * (dot_nt(g, global_values) - delta)).astype(BF16)
        far_g = jnp.concatenate([dot_nt(g[rows[j]], picked_values[j]) for j in range(BLOCKS)], axis=0)
        far_d = (far * (far_g - delta)).astype(BF16)
        change = dot_nn(near_d, keys) + dot_nn(glob_d, global_keys)
        change += jnp.concatenate([dot_nn(far_d[rows[j]], picked_keys[j]) for j in range(BLOCKS)], axis=0)
        grad_query[:, cols] = (change * scale).astype(BF16)
        near_key = dot_tn(near_d, q) * scale
        near_value = dot_tn(near_b, g)
        own_key[:, cols] = near_key[BLOCK : BLOCK + TOK]
        own_value[:, cols] = near_value[BLOCK : BLOCK + TOK]
        edge_out[0, :BLOCK, cols] = near_key[:BLOCK].astype(BF16)
        edge_out[0, BLOCK:, cols] = near_value[:BLOCK].astype(BF16)
        edge_out[1, :BLOCK, cols] = near_key[BLOCK + TOK :].astype(BF16)
        edge_out[1, BLOCK:, cols] = near_value[BLOCK + TOK :].astype(BF16)
        glob_key = (dot_tn(glob_d, q) * scale).astype(BF16)
        glob_value = dot_tn(glob_b, g).astype(BF16)
        for i in range(GROUPS):
            tiles_out[i * 2 * HEADS + h] = glob_key[i * TILE : (i + 1) * TILE]
            tiles_out[i * 2 * HEADS + HEADS + h] = glob_value[i * TILE : (i + 1) * TILE]
        for j in range(BLOCKS):
            far_key = (dot_tn(far_d[rows[j]], q[rows[j]]) * scale).astype(BF16)
            far_value = dot_tn(far_b[rows[j]], g[rows[j]]).astype(BF16)
            for p in range(PICKS):
                slot = table[at(j, p)]
                slots_out[slot, :BLOCK] = far_key[p * BLOCK : (p + 1) * BLOCK]
                slots_out[slot, BLOCK:] = far_value[p * BLOCK : (p + 1) * BLOCK]


def collect_kernel(last_device, want, count, pos, own_key, own_value, edge, tiles, slots, grad_key, grad_value, total):
    me = count[count.shape[0] - 1]
    for j in range(BLOCKS):
        for h in range(HEADS):
            rows, cols = pl.ds(j * BLOCK, BLOCK), pl.ds(h * DIM, DIM)
            total[j * HEADS + h, :BLOCK] = own_key[rows, cols]
            total[j * HEADS + h, BLOCK:] = own_value[rows, cols]

    @pl.loop(0, slots.shape[0])
    def _(k):
        @pl.when(count[k] > 0)
        def _():
            total[want[k]] += slots[k].astype(F32)

    from_left = jnp.where(me == 0, 0.0, 1.0)
    from_right = jnp.where(me == last_device, 0.0, 1.0)
    hot = (lax.broadcasted_iota(jnp.int32, (TOK, GLOB), 0) == pos[...] - me * TOK).astype(F32).astype(BF16)
    for h in range(HEADS):
        cols = pl.ds(h * DIM, DIM)
        for c, out in enumerate((grad_key, grad_value)):
            part = pl.ds(c * BLOCK, BLOCK)
            glob = jnp.concatenate([tiles[i * 2 * HEADS + c * HEADS + h] for i in range(GROUPS)], axis=0)
            placed = dot_nn(hot, glob)
            for j in range(BLOCKS):
                whole = total[j * HEADS + h, part] + placed[j * BLOCK : (j + 1) * BLOCK]
                if j == 0:
                    whole += edge[0, part, cols].astype(F32) * from_left
                if j == BLOCKS - 1:
                    whole += edge[1, part, cols].astype(F32) * from_right
                out[pl.ds(j * BLOCK, BLOCK), cols] = whole.astype(BF16)


def body(query_rows, key_rows, value_rows, grad_out, rand_blocks, global_pos):
    size = lax.axis_size("seq")
    me = lax.axis_index("seq")
    query, key, value, grad = (a.reshape(TOK, COLS) for a in (query_rows, key_rows, value_rows, grad_out))
    picks = rand_blocks.reshape(HEADS, size, BLOCKS * PICKS)
    mine = lax.dynamic_slice_in_dim(picks, me, 1, 1).reshape(HEADS * BLOCKS * PICKS)
    table = jnp.concatenate([mine // BLOCKS, me[None]])
    named = (picks // BLOCKS == me).astype(jnp.int32)
    code = picks % BLOCKS * HEADS + jnp.arange(HEADS)[:, None, None]
    want = jnp.sum(named * code, axis=(0, 2))
    count = jnp.concatenate([jnp.sum(named, axis=(0, 2)), me[None]])

    shape = jax.ShapeDtypeStruct
    slot_shape, tile_shape, edge_shape = (size, 2 * BLOCK, DIM), (size, TILE, DIM), (2, 2 * BLOCK, COLS)
    comm_scratch = [
        pltpu.VMEM(tile_shape, BF16),
        pltpu.VMEM((TILE, DIM), BF16),
        pltpu.SemaphoreType.DMA((2, 4)),
        pltpu.SemaphoreType.DMA((2,)),
        pltpu.SemaphoreType.DMA((2,)),
        pltpu.SemaphoreType.DMA((2,)),
    ]
    slots, edge, tiles = pl.pallas_call(
        functools.partial(fetch_kernel, size),
        out_shape=[shape(slot_shape, BF16), shape(edge_shape, BF16), shape(tile_shape, BF16)],
        in_specs=[SMEM, VMEM, VMEM, VMEM],
        out_specs=[VMEM] * 3,
        scratch_shapes=[
            pltpu.VMEM((BLOCKS * HEADS, 2 * BLOCK, DIM), BF16),
            pltpu.VMEM(slot_shape, BF16),
            pltpu.VMEM(tile_shape, BF16),
            *comm_scratch,
        ],
        compiler_params=pltpu.CompilerParams(
            collective_id=0, has_side_effects=True, vmem_limit_bytes=32 << 20
        ),
        name="fetch",
    )(want, global_pos[:, None], key, value)
    wide = shape((TOK, COLS), F32)
    narrow = shape((TOK, COLS), BF16)
    attended, grad_query, own_key, own_value, edge_grads, tile_grads, slot_grads = pl.pallas_call(
        functools.partial(attention_kernel, size - 1),
        out_shape=[narrow, narrow, wide, wide, shape(edge_shape, BF16), shape(tile_shape, BF16), shape(slot_shape, BF16)],
        in_specs=[SMEM] + [VMEM] * 7,
        out_specs=[VMEM] * 7,
        compiler_params=pltpu.CompilerParams(vmem_limit_bytes=32 << 20),
        name="attention",
    )(table, query, key, value, grad, edge, tiles, slots)
    edge_back, tiles_back, slots_back = pl.pallas_call(
        functools.partial(return_kernel, size),
        out_shape=[shape(edge_shape, BF16), shape(tile_shape, BF16), shape(slot_shape, BF16)],
        in_specs=[VMEM] * 3,
        out_specs=[VMEM] * 3,
        scratch_shapes=comm_scratch,
        compiler_params=pltpu.CompilerParams(
            collective_id=1, has_side_effects=True, vmem_limit_bytes=32 << 20
        ),
        name="give_back",
    )(edge_grads, tile_grads, slot_grads)
    grad_key, grad_value = pl.pallas_call(
        functools.partial(collect_kernel, size - 1),
        out_shape=[narrow, narrow],
        in_specs=[SMEM, SMEM] + [VMEM] * 6,
        out_specs=[VMEM] * 2,
        scratch_shapes=[pltpu.VMEM((BLOCKS * HEADS, 2 * BLOCK, DIM), F32)],
        compiler_params=pltpu.CompilerParams(vmem_limit_bytes=32 << 20),
        name="collect",
    )(want, count, global_pos[None, :], own_key, own_value, edge_back, tiles_back, slots_back)
    return tuple(a.reshape(1, TOK, COLS) for a in (attended, grad_query, grad_key, grad_value))


def solution(mesh):
    rows = P(None, "seq", "head")
    return jax.shard_map(
        body,
        mesh=mesh,
        in_specs=(rows, rows, rows, rows, P(None, "head", None, None), P()),
        out_specs=(rows, rows, rows, rows),
        check_vma=False,
    )
```

```python
import functools

import jax
import jax.numpy as jnp
from jax import lax
from jax.experimental import pallas as pl
from jax.experimental.pallas import tpu as pltpu
from jax.sharding import PartitionSpec as P

BLOCK = 64
DIM = 128
HEADS = 4
BLOCKS = 4
PICKS = 3
TOK = BLOCK * BLOCKS
COLS = HEADS * DIM
GLOB = 128
TILE = 16
GROUPS = GLOB // TILE
SEQ = 64
RING = 8
NPICK = HEADS * BLOCKS * PICKS
WIDE = (BLOCKS + 2) * BLOCK
FAR = PICKS * BLOCK
SCALE = DIM**-0.5
CHUNKS = (1, 9, 17, 25, SEQ)
BF16 = jnp.bfloat16
F32 = jnp.float32
MESH = pl.DeviceIdType.MESH
VMEM = pl.BlockSpec(memory_space=pltpu.VMEM)
SMEM = pl.BlockSpec(memory_space=pltpu.SMEM)
ANY = pl.BlockSpec(memory_space=pl.ANY)
UPPER, LOWER = pl.ds(0, BLOCK), pl.ds(BLOCK, BLOCK)


def send_to(peer, src, dst, sems):
    return pltpu.make_async_remote_copy(
        src_ref=src,
        dst_ref=dst,
        send_sem=sems.at[0],
        recv_sem=sems.at[1],
        device_id={"seq": peer},
        device_id_type=MESH,
    )


def dot_nt(a, b):
    return lax.dot_general(a, b, (((1,), (1,)), ((), ())), preferred_element_type=F32)


def dot_tn(a, b):
    return lax.dot_general(a, b, (((0,), (0,)), ((), ())), preferred_element_type=F32)


def dot_nn(a, b):
    return jnp.dot(a, b, preferred_element_type=F32)


class Tiles:
    def __init__(self, me, tiles, part, middle, piece, row, out, sems):
        self.z, self.xc = me // 2 % RING, me // (2 * RING) * 2 + me % 2
        self.tiles, self.part, self.middle, self.piece, self.row, self.out = tiles, part, middle, piece, row, out
        self.sems = sems

    def along_xc(self, k):
        other = lax.rem(self.xc + k, RING)
        return other, (other // 2 * RING + self.z) * 2 + other % 2

    def along_z(self, k):
        other = lax.rem(self.z + k, RING)
        return other, (self.xc // 2 * RING + other) * 2 + self.xc % 2

    def start_first(self):
        for k in range(1, RING):
            other, peer = self.along_xc(k)
            send_to(peer, self.tiles.at[other], self.part.at[self.xc], self.sems.at[0]).start()
        self.part[self.xc] = self.tiles[self.xc]

    def start_second(self):
        rest = pl.ds(0, RING - 1)
        send_to(self.along_xc(1)[1], self.tiles.at[rest], self.part.at[rest], self.sems.at[0]).wait()
        self.middle[...] = jnp.sum(self.part[...].astype(F32), axis=0).astype(BF16)
        for k in range(1, RING):
            other, peer = self.along_z(k)
            send_to(peer, self.middle.at[other], self.piece.at[self.z], self.sems.at[1]).start()
        self.piece[self.z] = self.middle[self.z]

    def start_third(self):
        rest = pl.ds(0, RING - 1)
        send_to(self.along_z(1)[1], self.middle.at[rest], self.piece.at[rest], self.sems.at[1]).wait()
        self.row[self.z] = jnp.sum(self.piece[...].astype(F32), axis=0).astype(BF16)
        for k in range(1, RING):
            _, peer = self.along_z(k)
            send_to(peer, self.row.at[self.z], self.row.at[self.z], self.sems.at[2]).start()

    def start_fourth(self):
        rest = pl.ds(0, RING - 1)
        send_to(self.along_z(1)[1], self.row.at[rest], self.row.at[rest], self.sems.at[2]).wait()
        for k in range(1, RING):
            _, peer = self.along_xc(k)
            send_to(peer, self.row, self.out.at[self.xc], self.sems.at[3]).start()
        self.out[self.xc] = self.row[...]

    def finish(self):
        rest = pl.ds(0, RING - 1)
        send_to(self.along_xc(1)[1], self.tiles.at[rest], self.out.at[rest], self.sems.at[3]).wait()


def main_kernel(
    tables, pos, query_hbm, key_hbm, value_hbm, grad_hbm,
    attended, grad_query, own_key, own_value, edge_back, tiles_back, slots_back,
    query, key, value, grad, stacked, slots_out, slots, edge, tiles_in, part, middle, piece, row, tiles,
    near_s, near_g, glob_s, glob_g, near_p, near_d, glob_d, glob_p, far_s, picked,
    edge_grads, back_in, back_part, back_middle, back_piece, back_row, back_out,
    local_sems, edge_sems, tile_sems, slot_sems, edge_back_sems, tile_back_sems, slot_back_sems,
):
    me = lax.axis_index("seq")
    right, left = lax.rem(me + 1, SEQ), lax.rem(me + SEQ - 1, SEQ)
    want = lambda k: tables[k]
    given = lambda k: tables[SEQ + k]
    holder = lambda h, j, p: tables[2 * SEQ + (h * BLOCKS + j) * PICKS + p]
    barrier = pltpu.get_barrier_semaphore()

    @pl.loop(1, SEQ)
    def _(k):
        pl.semaphore_signal(barrier, inc=1, device_id={"seq": lax.rem(me + k, SEQ)}, device_id_type=MESH)

    loads = [
        pltpu.make_async_copy(src, dst, local_sems.at[i])
        for i, (src, dst) in enumerate(((key_hbm, key), (value_hbm, value), (query_hbm, query), (grad_hbm, grad)))
    ]
    for copy in loads:
        copy.start()
    loads[0].wait()
    loads[1].wait()

    for j in range(BLOCKS):
        for h in range(HEADS):
            rows, cols = pl.ds(j * BLOCK, BLOCK), pl.ds(h * DIM, DIM)
            stacked[j * HEADS + h, UPPER] = key[rows, cols]
            stacked[j * HEADS + h, LOWER] = value[rows, cols]
    hot = (lax.broadcasted_iota(jnp.int32, (TOK, GLOB), 0) == pos[...] - me * TOK).astype(F32).astype(BF16)
    for c, ref in enumerate((key, value)):
        owned = dot_tn(hot, ref[...]).astype(BF16)
        for g in range(GROUPS):
            for h in range(HEADS):
                tiles_in[g, c * HEADS + h] = owned[g * TILE : (g + 1) * TILE, h * DIM : (h + 1) * DIM]

    def fill_slot(k):
        slots_out[k] = stacked[want(k)]

    @pl.loop(0, SEQ)
    def _(k):
        fill_slot(k)

    slots[me] = slots_out[me]

    def send_slots(chunk):
        @pl.loop(CHUNKS[chunk], CHUNKS[chunk + 1])
        def _(k):
            peer = lax.rem(me + k, SEQ)
            send_to(peer, slots_out.at[peer], slots.at[me], slot_sems).start()

    pl.semaphore_wait(barrier, SEQ - 1)
    last, first = pl.ds(TOK - BLOCK, BLOCK), pl.ds(0, BLOCK)
    edges = [
        send_to(left, key.at[first], edge.at[1, UPPER], edge_sems.at[0]),
        send_to(left, value.at[first], edge.at[1, LOWER], edge_sems.at[1]),
        send_to(right, key.at[last], edge.at[0, UPPER], edge_sems.at[2]),
        send_to(right, value.at[last], edge.at[0, LOWER], edge_sems.at[3]),
    ]
    shared = Tiles(me, tiles_in, part, middle, piece, row, tiles, tile_sems)
    shared.start_first()
    for copy in edges:
        copy.start()
    send_slots(0)
    shared.start_second()
    send_slots(1)
    shared.start_third()
    send_slots(2)
    shared.start_fourth()
    send_slots(3)

    loads[2].wait()
    loads[3].wait()
    for copy in edges:
        copy.wait()
    query_block = lax.broadcasted_iota(jnp.int32, (TOK, WIDE), 0) // BLOCK
    key_block = lax.broadcasted_iota(jnp.int32, (TOK, WIDE), 1) // BLOCK
    low = jnp.where(me == 0, 1, 0)
    high = jnp.where(me == SEQ - 1, BLOCKS, BLOCKS + 1)
    offset = key_block - query_block
    band = (offset >= 0) & (offset <= 2) & (key_block >= low) & (key_block <= high)

    def near_keys(cols):
        return jnp.concatenate([edge[0, UPPER, cols], key[:, cols], edge[1, UPPER, cols]], axis=0)

    def near_values(cols):
        return jnp.concatenate([edge[0, LOWER, cols], value[:, cols], edge[1, LOWER, cols]], axis=0)

    def glob_keys(h):
        return jnp.concatenate([tiles[g, h] for g in range(GROUPS)], axis=0)

    def glob_values(h):
        return jnp.concatenate([tiles[g, HEADS + h] for g in range(GROUPS)], axis=0)

    for h in range(HEADS):
        cols = pl.ds(h * DIM, DIM)
        near_s[h] = jnp.where(band, dot_nt(query[:, cols], near_keys(cols)) * SCALE, -1e30)
        near_g[h] = dot_nt(grad[:, cols], near_values(cols))
    shared.finish()
    for h in range(HEADS):
        cols = pl.ds(h * DIM, DIM)
        glob_s[h] = dot_nt(query[:, cols], glob_keys(h)) * SCALE
        glob_g[h] = dot_nt(grad[:, cols], glob_values(h))
    rest = pl.ds(0, SEQ - 1)
    send_to(right, slots_out.at[rest], slots.at[rest], slot_sems).wait()

    block_rows = [slice(j * BLOCK, (j + 1) * BLOCK) for j in range(BLOCKS)]
    picked[NPICK] = jnp.zeros((2 * BLOCK, DIM), BF16)
    for h in range(HEADS):
        cols = pl.ds(h * DIM, DIM)
        q, g = query[:, cols], grad[:, cols]
        keys = [jnp.concatenate([slots[holder(h, j, p), UPPER] for p in range(PICKS)], axis=0) for j in range(BLOCKS)]
        values = [jnp.concatenate([slots[holder(h, j, p), LOWER] for p in range(PICKS)], axis=0) for j in range(BLOCKS)]
        far = jnp.concatenate([dot_nt(q[block_rows[j]], keys[j]) for j in range(BLOCKS)], axis=0) * SCALE
        near, glob = near_s[h], glob_s[h]
        row_max = jnp.maximum(
            jnp.max(near, axis=1, keepdims=True),
            jnp.maximum(jnp.max(far, axis=1, keepdims=True), jnp.max(glob, axis=1, keepdims=True)),
        )
        near, far, glob = jnp.exp(near - row_max), jnp.exp(far - row_max), jnp.exp(glob - row_max)
        total = (
            jnp.sum(near, axis=1, keepdims=True)
            + jnp.sum(far, axis=1, keepdims=True)
            + jnp.sum(glob, axis=1, keepdims=True)
        )
        inverse = 1.0 / total
        near, far, glob = near * inverse, far * inverse, glob * inverse
        near_b, far_b, glob_b = near.astype(BF16), far.astype(BF16), glob.astype(BF16)
        mixed = dot_nn(near_b, near_values(cols)) + dot_nn(glob_b, glob_values(h))
        mixed += jnp.concatenate([dot_nn(far_b[block_rows[j]], values[j]) for j in range(BLOCKS)], axis=0)
        attended[:, cols] = mixed.astype(BF16)
        delta = jnp.sum(g.astype(F32) * mixed, axis=1, keepdims=True)
        far_g = jnp.concatenate([dot_nt(g[block_rows[j]], values[j]) for j in range(BLOCKS)], axis=0)
        far_d = (far * (far_g - delta)).astype(BF16)
        for j in range(BLOCKS):
            far_key = (dot_tn(far_d[block_rows[j]], q[block_rows[j]]) * SCALE).astype(BF16)
            far_value = dot_tn(far_b[block_rows[j]], g[block_rows[j]]).astype(BF16)
            for p in range(PICKS):
                at = (h * BLOCKS + j) * PICKS + p
                picked[at, UPPER] = far_key[p * BLOCK : (p + 1) * BLOCK]
                picked[at, LOWER] = far_value[p * BLOCK : (p + 1) * BLOCK]
        far_s[h] = jnp.concatenate([dot_nn(far_d[block_rows[j]], keys[j]) for j in range(BLOCKS)], axis=0)
        near_p[h] = near_b
        glob_p[h] = glob_b
        near_d[h] = (near * (near_g[h] - delta)).astype(BF16)
        glob_d[h] = (glob * (glob_g[h] - delta)).astype(BF16)

    def return_slots(chunk):
        @pl.loop(CHUNKS[chunk], CHUNKS[chunk + 1])
        def _(k):
            peer = lax.rem(me + k, SEQ)
            slots_out[peer] = picked[given(peer)]
            send_to(peer, slots_out.at[peer], slots_back.at[me], slot_back_sems).start()

    for h in range(HEADS):
        cols = pl.ds(h * DIM, DIM)
        glob_key = (dot_tn(glob_d[h], query[:, cols]) * SCALE).astype(BF16)
        glob_value = dot_tn(glob_p[h], grad[:, cols]).astype(BF16)
        for g in range(GROUPS):
            back_in[g, h] = glob_key[g * TILE : (g + 1) * TILE]
            back_in[g, HEADS + h] = glob_value[g * TILE : (g + 1) * TILE]
    summed = Tiles(me, back_in, back_part, back_middle, back_piece, back_row, back_out, tile_back_sems)
    summed.start_first()
    return_slots(0)
    slots_back[me] = picked[given(me)]
    for h in range(HEADS):
        cols = pl.ds(h * DIM, DIM)
        q, g = query[:, cols], grad[:, cols]
        near_key = dot_tn(near_d[h], q) * SCALE
        near_value = dot_tn(near_p[h], g)
        own_key[:, cols] = near_key[BLOCK : BLOCK + TOK]
        own_value[:, cols] = near_value[BLOCK : BLOCK + TOK]
        edge_grads[0, UPPER, cols] = near_key[:BLOCK].astype(BF16)
        edge_grads[0, LOWER, cols] = near_value[:BLOCK].astype(BF16)
        edge_grads[1, UPPER, cols] = near_key[BLOCK + TOK :].astype(BF16)
        edge_grads[1, LOWER, cols] = near_value[BLOCK + TOK :].astype(BF16)
    edges = [
        send_to(left, edge_grads.at[0], edge_back.at[1], edge_back_sems.at[0]),
        send_to(right, edge_grads.at[1], edge_back.at[0], edge_back_sems.at[1]),
    ]
    for copy in edges:
        copy.start()
    summed.start_second()
    return_slots(1)
    summed.start_third()
    return_slots(2)
    summed.start_fourth()
    return_slots(3)
    for h in range(HEADS):
        cols = pl.ds(h * DIM, DIM)
        change = dot_nn(near_d[h], near_keys(cols)) + dot_nn(glob_d[h], glob_keys(h)) + far_s[h]
        grad_query[:, cols] = (change * SCALE).astype(BF16)
    summed.finish()
    tiles_back[...] = back_out[...]
    for copy in edges:
        copy.wait()
    send_to(right, slots_out.at[rest], slots_back.at[rest], slot_back_sems).wait()


def collect_kernel(tables, pos, own_key, own_value, edge, tiles, slots, grad_key, grad_value, total):
    me = tables[2 * SEQ + NPICK]
    for j in range(BLOCKS):
        for h in range(HEADS):
            rows, cols = pl.ds(j * BLOCK, BLOCK), pl.ds(h * DIM, DIM)
            total[j * HEADS + h, UPPER] = own_key[rows, cols]
            total[j * HEADS + h, LOWER] = own_value[rows, cols]

    @pl.loop(0, SEQ)
    def _(k):
        total[tables[k]] += slots[k].astype(F32)

    from_left = jnp.where(me == 0, 0.0, 1.0)
    from_right = jnp.where(me == SEQ - 1, 0.0, 1.0)
    hot = (lax.broadcasted_iota(jnp.int32, (TOK, GLOB), 0) == pos[...] - me * TOK).astype(F32).astype(BF16)
    for h in range(HEADS):
        cols = pl.ds(h * DIM, DIM)
        for c, out in enumerate((grad_key, grad_value)):
            part = pl.ds(c * BLOCK, BLOCK)
            glob = jnp.concatenate([tiles[g, c * HEADS + h] for g in range(GROUPS)], axis=0)
            placed = dot_nn(hot, glob)
            for j in range(BLOCKS):
                whole = total[j * HEADS + h, part] + placed[j * BLOCK : (j + 1) * BLOCK]
                if j == 0:
                    whole += edge[0, part, cols].astype(F32) * from_left
                if j == BLOCKS - 1:
                    whole += edge[1, part, cols].astype(F32) * from_right
                out[pl.ds(j * BLOCK, BLOCK), cols] = whole.astype(BF16)


def make_tables(rand_blocks, me):
    picks = rand_blocks.reshape(HEADS, SEQ, BLOCKS * PICKS)
    holders = picks // BLOCKS
    code = picks % BLOCKS * HEADS + jnp.arange(HEADS)[:, None, None]
    want = jnp.sum(jnp.where(holders == me, code, 0), axis=(0, 2))
    mine = lax.dynamic_slice_in_dim(holders, me, 1, 1).reshape(NPICK)
    index = jnp.arange(NPICK)[None, :] - NPICK
    given = NPICK + jnp.sum(jnp.where(mine[None, :] == jnp.arange(SEQ)[:, None], index, 0), axis=1)
    return jnp.concatenate([want, given, mine, me[None]])


def body(query_rows, key_rows, value_rows, grad_out, rand_blocks, global_pos):
    me = lax.axis_index("seq")
    arrays = [a.reshape(TOK, COLS) for a in (query_rows, key_rows, value_rows, grad_out)]
    tables = make_tables(rand_blocks, me)
    pos = global_pos[None, :]
    shape = jax.ShapeDtypeStruct
    slot_shape, edge_shape = (SEQ, 2 * BLOCK, DIM), (2, 2 * BLOCK, COLS)
    grid_shape, row_shape = (RING, RING, TILE, DIM), (RING, TILE, DIM)
    wide, narrow = shape((TOK, COLS), F32), shape((TOK, COLS), BF16)
    bf16 = lambda dims: pltpu.VMEM(dims, BF16)
    f32 = lambda dims: pltpu.VMEM(dims, F32)
    dma = pltpu.SemaphoreType.DMA
    tile_scratch = [bf16(grid_shape), bf16(grid_shape), bf16(row_shape), bf16(row_shape), bf16(row_shape), bf16(grid_shape)]
    attended, grad_query, own_key, own_value, edge, tiles, slots = pl.pallas_call(
        main_kernel,
        out_shape=[narrow, narrow, wide, wide, shape(edge_shape, BF16), shape(grid_shape, BF16), shape(slot_shape, BF16)],
        in_specs=[SMEM, VMEM, ANY, ANY, ANY, ANY],
        out_specs=[VMEM] * 7,
        scratch_shapes=[
            *[bf16((TOK, COLS))] * 4,
            bf16((BLOCKS * HEADS, 2 * BLOCK, DIM)),
            bf16(slot_shape),
            bf16(slot_shape),
            bf16(edge_shape),
            *tile_scratch,
            f32((HEADS, TOK, WIDE)),
            f32((HEADS, TOK, WIDE)),
            f32((HEADS, TOK, GLOB)),
            f32((HEADS, TOK, GLOB)),
            bf16((HEADS, TOK, WIDE)),
            bf16((HEADS, TOK, WIDE)),
            bf16((HEADS, TOK, GLOB)),
            bf16((HEADS, TOK, GLOB)),
            f32((HEADS, TOK, DIM)),
            bf16((NPICK + 1, 2 * BLOCK, DIM)),
            bf16(edge_shape),
            *tile_scratch,
            dma((4,)),
            dma((4, 2)),
            dma((4, 2)),
            dma((2,)),
            dma((2, 2)),
            dma((4, 2)),
            dma((2,)),
        ],
        compiler_params=pltpu.CompilerParams(
            collective_id=0, has_side_effects=True, vmem_limit_bytes=48 << 20
        ),
        name="attend",
    )(tables, pos, *arrays)
    grad_key, grad_value = pl.pallas_call(
        collect_kernel,
        out_shape=[narrow, narrow],
        in_specs=[SMEM] + [VMEM] * 6,
        out_specs=[VMEM] * 2,
        scratch_shapes=[f32((BLOCKS * HEADS, 2 * BLOCK, DIM))],
        compiler_params=pltpu.CompilerParams(vmem_limit_bytes=32 << 20),
        name="collect",
    )(tables, pos, own_key, own_value, edge, tiles, slots)
    return tuple(a.reshape(1, TOK, COLS) for a in (attended, grad_query, grad_key, grad_value))


def solution(mesh):
    rows = P(None, "seq", "head")
    return jax.shard_map(
        body,
        mesh=mesh,
        in_specs=(rows, rows, rows, rows, P(None, "head", None, None), P()),
        out_specs=(rows, rows, rows, rows),
        check_vma=False,
    )
```

```python
import functools

import jax
import jax.numpy as jnp
from jax import lax
from jax.experimental import pallas as pl
from jax.experimental.pallas import tpu as pltpu
from jax.sharding import PartitionSpec as P

BLOCK = 64
DIM = 128
HEADS = 4
BLOCKS = 4
PICKS = 3
TOK = BLOCK * BLOCKS
COLS = HEADS * DIM
GLOB = 128
TILE = 16
GROUPS = GLOB // TILE
SEQ = 64
RING = 8
NPICK = HEADS * BLOCKS * PICKS
WIDE = (BLOCKS + 2) * BLOCK
FAR = PICKS * BLOCK
SCALE = DIM**-0.5
CHUNKS = (1, 21, 33, 45, SEQ)
EARLY = 5
MINE = 1
BF16 = jnp.bfloat16
F32 = jnp.float32
MESH = pl.DeviceIdType.MESH
VMEM = pl.BlockSpec(memory_space=pltpu.VMEM)
SMEM = pl.BlockSpec(memory_space=pltpu.SMEM)
ANY = pl.BlockSpec(memory_space=pl.ANY)
UPPER, LOWER = pl.ds(0, BLOCK), pl.ds(BLOCK, BLOCK)


def send_to(peer, src, dst, sems):
    return pltpu.make_async_remote_copy(
        src_ref=src,
        dst_ref=dst,
        send_sem=sems.at[0],
        recv_sem=sems.at[1],
        device_id={"seq": peer},
        device_id_type=MESH,
    )


def dot_nt(a, b):
    return lax.dot_general(a, b, (((1,), (1,)), ((), ())), preferred_element_type=F32)


def dot_tn(a, b):
    return lax.dot_general(a, b, (((0,), (0,)), ((), ())), preferred_element_type=F32)


def dot_nn(a, b):
    return jnp.dot(a, b, preferred_element_type=F32)


def named_by(table, device):
    at = device * BLOCKS
    return jnp.maximum(
        jnp.maximum(table[0, at], table[0, at + 1]), jnp.maximum(table[0, at + 2], table[0, at + 3])
    )


class Tiles:
    def __init__(self, me, tiles, part, middle, piece, row, out, sems):
        self.z, self.xc = me // 2 % RING, me // (2 * RING) * 2 + me % 2
        self.tiles, self.part, self.middle, self.piece, self.row, self.out = tiles, part, middle, piece, row, out
        self.sems = sems

    def along_xc(self, k):
        other = lax.rem(self.xc + k, RING)
        return other, (other // 2 * RING + self.z) * 2 + other % 2

    def along_z(self, k):
        other = lax.rem(self.z + k, RING)
        return other, (self.xc // 2 * RING + other) * 2 + self.xc % 2

    def start_first(self):
        for k in range(1, RING):
            other, peer = self.along_xc(k)
            send_to(peer, self.tiles.at[other], self.part.at[self.xc], self.sems.at[0]).start()
        self.part[self.xc] = self.tiles[self.xc]

    def start_second(self):
        rest = pl.ds(0, RING - 1)
        send_to(self.along_xc(1)[1], self.tiles.at[rest], self.part.at[rest], self.sems.at[0]).wait()
        self.middle[...] = jnp.sum(self.part[...].astype(F32), axis=0).astype(BF16)
        for k in range(1, RING):
            other, peer = self.along_z(k)
            send_to(peer, self.middle.at[other], self.piece.at[self.z], self.sems.at[1]).start()
        self.piece[self.z] = self.middle[self.z]

    def start_third(self):
        rest = pl.ds(0, RING - 1)
        send_to(self.along_z(1)[1], self.middle.at[rest], self.piece.at[rest], self.sems.at[1]).wait()
        self.row[self.z] = jnp.sum(self.piece[...].astype(F32), axis=0).astype(BF16)
        for k in range(1, RING):
            _, peer = self.along_z(k)
            send_to(peer, self.row.at[self.z], self.row.at[self.z], self.sems.at[2]).start()

    def start_fourth(self):
        rest = pl.ds(0, RING - 1)
        send_to(self.along_z(1)[1], self.row.at[rest], self.row.at[rest], self.sems.at[2]).wait()
        for k in range(1, RING):
            _, peer = self.along_xc(k)
            send_to(peer, self.row, self.out.at[self.xc], self.sems.at[3]).start()
        self.out[self.xc] = self.row[...]

    def finish(self):
        rest = pl.ds(0, RING - 1)
        send_to(self.along_xc(1)[1], self.tiles.at[rest], self.out.at[rest], self.sems.at[3]).wait()


def main_kernel(
    query_hbm, key_hbm, value_hbm, grad_hbm, rand_hbm, pos_hbm,
    attended, grad_query, own_key, own_value, edge_back, tiles_back, slots_back, table,
    rand, rand_smem, pos, table_smem, given_vmem, given_smem, query, key, value, grad, stacked, slots_out, slots, edge, tiles_in, part, middle, piece, row, tiles,
    near_s, near_g, glob_s, glob_g, near_p, near_d, glob_d, glob_p, far_d, row_max, row_sum, picked,
    edge_grads, back_in, back_part, back_middle, back_piece, back_row, back_out,
    local_sems, edge_sems, tile_sems, slot_sems, edge_back_sems, tile_back_sems, slot_back_sems,
):
    me = lax.axis_index("seq")
    right, left = lax.rem(me + 1, SEQ), lax.rem(me + SEQ - 1, SEQ)
    barrier = pltpu.get_barrier_semaphore()
    loads = [
        pltpu.make_async_copy(src, dst, local_sems.at[i])
        for i, (src, dst) in enumerate(
            (
                (rand_hbm, rand),
                (rand_hbm, rand_smem),
                (pos_hbm, pos),
                (key_hbm, key),
                (value_hbm, value),
                (query_hbm, query),
                (grad_hbm, grad),
            )
        )
    ]
    for copy in loads:
        copy.start()

    @pl.loop(1, SEQ)
    def _(k):
        pl.semaphore_signal(barrier, inc=1, device_id={"seq": lax.rem(me + k, SEQ)}, device_id_type=MESH)

    for copy in loads[:5]:
        copy.wait()

    asked = jnp.zeros((HEADS, SEQ * BLOCKS), jnp.int32)
    for p in range(PICKS):
        names = rand[p]
        code = (names & (BLOCKS - 1)) * HEADS + lax.broadcasted_iota(jnp.int32, names.shape, 0)
        asked = jnp.maximum(asked, jnp.where(names >> 2 == me, code, 0))
    asked = jnp.max(asked, axis=0, keepdims=True)
    line = lax.broadcasted_iota(jnp.int32, (8, SEQ * BLOCKS), 0)
    table[...] = jnp.where(line == MINE, me, asked)
    holder = lambda h, j, p: rand_smem[p, h, me * BLOCKS + j] >> 2
    lane = lax.broadcasted_iota(jnp.int32, (8, DIM), 1)
    found = jnp.full((8, DIM), NPICK, jnp.int32)
    for h in range(HEADS):
        for j in range(BLOCKS):
            for p in range(PICKS):
                found = jnp.where(lane == holder(h, j, p), (h * BLOCKS + j) * PICKS + p, found)
    given_vmem[...] = found
    copies = [
        pltpu.make_async_copy(table, table_smem, local_sems.at[7]),
        pltpu.make_async_copy(given_vmem, given_smem, local_sems.at[8]),
    ]
    for copy in copies:
        copy.start()
    given = lambda k: given_smem[0, k]
    want = lambda k: named_by(table_smem, k)

    for j in range(BLOCKS):
        for h in range(HEADS):
            rows, cols = pl.ds(j * BLOCK, BLOCK), pl.ds(h * DIM, DIM)
            stacked[j * HEADS + h, UPPER] = key[rows, cols]
            stacked[j * HEADS + h, LOWER] = value[rows, cols]
    hot = (lax.broadcasted_iota(jnp.int32, (TOK, GLOB), 0) == pos[...] - me * TOK).astype(F32).astype(BF16)
    for c, ref in enumerate((key, value)):
        owned = dot_tn(hot, ref[...]).astype(BF16)
        for g in range(GROUPS):
            for h in range(HEADS):
                tiles_in[g, c * HEADS + h] = owned[g * TILE : (g + 1) * TILE, h * DIM : (h + 1) * DIM]

    for copy in copies:
        copy.wait()

    @pl.loop(0, SEQ)
    def _(k):
        slots_out[k] = stacked[want(k)]

    slots[me] = slots_out[me]

    def send_slots(chunk):
        @pl.loop(CHUNKS[chunk], CHUNKS[chunk + 1])
        def _(k):
            peer = lax.rem(me + k, SEQ)
            send_to(peer, slots_out.at[peer], slots.at[me], slot_sems).start()

    pl.semaphore_wait(barrier, SEQ - 1)
    last, first = pl.ds(TOK - BLOCK, BLOCK), pl.ds(0, BLOCK)
    edges = [
        send_to(left, key.at[first], edge.at[1, UPPER], edge_sems.at[0]),
        send_to(left, value.at[first], edge.at[1, LOWER], edge_sems.at[1]),
        send_to(right, key.at[last], edge.at[0, UPPER], edge_sems.at[2]),
        send_to(right, value.at[last], edge.at[0, LOWER], edge_sems.at[3]),
    ]
    shared = Tiles(me, tiles_in, part, middle, piece, row, tiles, tile_sems)
    shared.start_first()
    for copy in edges:
        copy.start()
    send_slots(0)
    shared.start_second()
    send_slots(1)
    shared.start_third()
    send_slots(2)
    shared.start_fourth()
    send_slots(3)

    loads[5].wait()
    loads[6].wait()
    for copy in edges:
        copy.wait()
    query_block = lax.broadcasted_iota(jnp.int32, (TOK, WIDE), 0) // BLOCK
    key_block = lax.broadcasted_iota(jnp.int32, (TOK, WIDE), 1) // BLOCK
    low = jnp.where(me == 0, 1, 0)
    high = jnp.where(me == SEQ - 1, BLOCKS, BLOCKS + 1)
    offset = key_block - query_block
    band = (offset >= 0) & (offset <= 2) & (key_block >= low) & (key_block <= high)

    def near_keys(cols):
        return jnp.concatenate([edge[0, UPPER, cols], key[:, cols], edge[1, UPPER, cols]], axis=0)

    def near_values(cols):
        return jnp.concatenate([edge[0, LOWER, cols], value[:, cols], edge[1, LOWER, cols]], axis=0)

    def glob_keys(h):
        return jnp.concatenate([tiles[g, h] for g in range(GROUPS)], axis=0)

    def glob_values(h):
        return jnp.concatenate([tiles[g, HEADS + h] for g in range(GROUPS)], axis=0)

    for h in range(HEADS):
        cols = pl.ds(h * DIM, DIM)
        near_s[h] = jnp.where(band, dot_nt(query[:, cols], near_keys(cols)) * SCALE, -1e30)
        near_g[h] = dot_nt(grad[:, cols], near_values(cols))
    shared.finish()
    for h in range(HEADS):
        cols = pl.ds(h * DIM, DIM)
        near, glob = near_s[h], dot_nt(query[:, cols], glob_keys(h)) * SCALE
        top = jnp.maximum(jnp.max(near, axis=1, keepdims=True), jnp.max(glob, axis=1, keepdims=True))
        near, glob = jnp.exp(near - top), jnp.exp(glob - top)
        near_s[h], glob_s[h] = near, glob
        row_max[h] = jnp.broadcast_to(top, (TOK, DIM))
        row_sum[h] = jnp.broadcast_to(
            jnp.sum(near, axis=1, keepdims=True) + jnp.sum(glob, axis=1, keepdims=True), (TOK, DIM)
        )
        glob_g[h] = dot_nt(grad[:, cols], glob_values(h))
    rest = pl.ds(0, SEQ - 1)
    send_to(right, slots_out.at[rest], slots.at[rest], slot_sems).wait()

    block_rows = [slice(j * BLOCK, (j + 1) * BLOCK) for j in range(BLOCKS)]
    picked[NPICK] = jnp.zeros((2 * BLOCK, DIM), BF16)

    def far_keys(h, j):
        return jnp.concatenate([slots[holder(h, j, p), UPPER] for p in range(PICKS)], axis=0)

    for h in range(HEADS):
        cols = pl.ds(h * DIM, DIM)
        q, g = query[:, cols], grad[:, cols]
        keys = [far_keys(h, j) for j in range(BLOCKS)]
        values = [jnp.concatenate([slots[holder(h, j, p), LOWER] for p in range(PICKS)], axis=0) for j in range(BLOCKS)]
        far = jnp.concatenate([dot_nt(q[block_rows[j]], keys[j]) for j in range(BLOCKS)], axis=0) * SCALE
        old_max, old_sum = row_max[h, :, :1], row_sum[h, :, :1]
        new_max = jnp.maximum(old_max, jnp.max(far, axis=1, keepdims=True))
        far = jnp.exp(far - new_max)
        shrink = jnp.exp(old_max - new_max)
        inverse = 1.0 / (old_sum * shrink + jnp.sum(far, axis=1, keepdims=True))
        near, far, glob = near_s[h] * (shrink * inverse), far * inverse, glob_s[h] * (shrink * inverse)
        near_b, far_b, glob_b = near.astype(BF16), far.astype(BF16), glob.astype(BF16)
        mixed = dot_nn(near_b, near_values(cols)) + dot_nn(glob_b, glob_values(h))
        mixed += jnp.concatenate([dot_nn(far_b[block_rows[j]], values[j]) for j in range(BLOCKS)], axis=0)
        attended[:, cols] = mixed.astype(BF16)
        delta = jnp.sum(g.astype(F32) * mixed, axis=1, keepdims=True)
        far_g = jnp.concatenate([dot_nt(g[block_rows[j]], values[j]) for j in range(BLOCKS)], axis=0)
        far_change = (far * (far_g - delta)).astype(BF16)
        far_d[h] = far_change
        for j in range(BLOCKS):
            far_key = (dot_tn(far_change[block_rows[j]], q[block_rows[j]]) * SCALE).astype(BF16)
            far_value = dot_tn(far_b[block_rows[j]], g[block_rows[j]]).astype(BF16)
            for p in range(PICKS):
                at = (h * BLOCKS + j) * PICKS + p
                picked[at, UPPER] = far_key[p * BLOCK : (p + 1) * BLOCK]
                picked[at, LOWER] = far_value[p * BLOCK : (p + 1) * BLOCK]
        near_p[h] = near_b
        glob_p[h] = glob_b
        near_d[h] = (near * (near_g[h] - delta)).astype(BF16)
        glob_d[h] = (glob * (glob_g[h] - delta)).astype(BF16)

    def return_slots(begin, end):
        @pl.loop(begin, end)
        def _(k):
            peer = lax.rem(me + k, SEQ)
            slots_out[peer] = picked[given(peer)]
            send_to(peer, slots_out.at[peer], slots_back.at[me], slot_back_sems).start()

    return_slots(CHUNKS[0], EARLY)
    for h in range(HEADS):
        cols = pl.ds(h * DIM, DIM)
        glob_key = (dot_tn(glob_d[h], query[:, cols]) * SCALE).astype(BF16)
        glob_value = dot_tn(glob_p[h], grad[:, cols]).astype(BF16)
        for g in range(GROUPS):
            back_in[g, h] = glob_key[g * TILE : (g + 1) * TILE]
            back_in[g, HEADS + h] = glob_value[g * TILE : (g + 1) * TILE]
    summed = Tiles(me, back_in, back_part, back_middle, back_piece, back_row, back_out, tile_back_sems)
    summed.start_first()
    return_slots(EARLY, CHUNKS[1])
    slots_back[me] = picked[given(me)]
    for h in range(HEADS):
        cols = pl.ds(h * DIM, DIM)
        q, g = query[:, cols], grad[:, cols]
        near_key = dot_tn(near_d[h], q) * SCALE
        near_value = dot_tn(near_p[h], g)
        own_key[:, cols] = near_key[BLOCK : BLOCK + TOK]
        own_value[:, cols] = near_value[BLOCK : BLOCK + TOK]
        edge_grads[0, UPPER, cols] = near_key[:BLOCK].astype(BF16)
        edge_grads[0, LOWER, cols] = near_value[:BLOCK].astype(BF16)
        edge_grads[1, UPPER, cols] = near_key[BLOCK + TOK :].astype(BF16)
        edge_grads[1, LOWER, cols] = near_value[BLOCK + TOK :].astype(BF16)
    edges = [
        send_to(left, edge_grads.at[0], edge_back.at[1], edge_back_sems.at[0]),
        send_to(right, edge_grads.at[1], edge_back.at[0], edge_back_sems.at[1]),
    ]
    for copy in edges:
        copy.start()
    summed.start_second()
    return_slots(CHUNKS[1], CHUNKS[2])
    summed.start_third()
    return_slots(CHUNKS[2], CHUNKS[3])
    summed.start_fourth()
    return_slots(CHUNKS[3], CHUNKS[4])
    for h in range(HEADS):
        cols = pl.ds(h * DIM, DIM)
        change = dot_nn(near_d[h], near_keys(cols)) + dot_nn(glob_d[h], glob_keys(h))
        change += jnp.concatenate([dot_nn(far_d[h, block_rows[j]], far_keys(h, j)) for j in range(BLOCKS)], axis=0)
        grad_query[:, cols] = (change * SCALE).astype(BF16)
    summed.finish()
    tiles_back[...] = back_out[...]
    for copy in edges:
        copy.wait()
    send_to(right, slots_out.at[rest], slots_back.at[rest], slot_back_sems).wait()


def collect_kernel(
    table, pos, attended_in, query_in, own_key, own_value, edge, tiles, slots,
    attended, grad_query, grad_key, grad_value, total,
):
    me = table[MINE, 0]
    attended[...] = attended_in[...]
    grad_query[...] = query_in[...]
    for j in range(BLOCKS):
        for h in range(HEADS):
            rows, cols = pl.ds(j * BLOCK, BLOCK), pl.ds(h * DIM, DIM)
            total[j * HEADS + h, UPPER] = own_key[rows, cols]
            total[j * HEADS + h, LOWER] = own_value[rows, cols]

    @pl.loop(0, SEQ)
    def _(k):
        total[named_by(table, k)] += slots[k].astype(F32)

    from_left = jnp.where(me == 0, 0.0, 1.0)
    from_right = jnp.where(me == SEQ - 1, 0.0, 1.0)
    hot = (lax.broadcasted_iota(jnp.int32, (TOK, GLOB), 0) == pos[...] - me * TOK).astype(F32).astype(BF16)
    for h in range(HEADS):
        cols = pl.ds(h * DIM, DIM)
        for c, out in enumerate((grad_key, grad_value)):
            part = pl.ds(c * BLOCK, BLOCK)
            glob = jnp.concatenate([tiles[g, c * HEADS + h] for g in range(GROUPS)], axis=0)
            placed = dot_nn(hot, glob)
            for j in range(BLOCKS):
                whole = total[j * HEADS + h, part] + placed[j * BLOCK : (j + 1) * BLOCK]
                if j == 0:
                    whole += edge[0, part, cols].astype(F32) * from_left
                if j == BLOCKS - 1:
                    whole += edge[1, part, cols].astype(F32) * from_right
                out[pl.ds(j * BLOCK, BLOCK), cols] = whole.astype(BF16)


def body(query_rows, key_rows, value_rows, grad_out, rand_blocks, global_pos):
    arrays = [a.reshape(TOK, COLS) for a in (query_rows, key_rows, value_rows, grad_out)]
    names = rand_blocks.transpose(0, 3, 1, 2).reshape(PICKS, HEADS, SEQ * BLOCKS)
    pos = global_pos[None, :]
    operands = [pltpu.with_memory_space_constraint(a, pltpu.HBM) for a in (*arrays, names, pos)]
    shape = jax.ShapeDtypeStruct
    slot_shape, edge_shape = (SEQ, 2 * BLOCK, DIM), (2, 2 * BLOCK, COLS)
    grid_shape, row_shape = (RING, RING, TILE, DIM), (RING, TILE, DIM)
    wide, narrow = shape((TOK, COLS), F32), shape((TOK, COLS), BF16)
    bf16 = lambda dims: pltpu.VMEM(dims, BF16)
    f32 = lambda dims: pltpu.VMEM(dims, F32)
    dma = pltpu.SemaphoreType.DMA
    tile_scratch = [bf16(grid_shape), bf16(grid_shape), bf16(row_shape), bf16(row_shape), bf16(row_shape), bf16(grid_shape)]
    attended, grad_query, own_key, own_value, edge, tiles, slots, table = pl.pallas_call(
        main_kernel,
        out_shape=[
            *[narrow, narrow, wide, wide],
            *[shape(dims, BF16) for dims in (edge_shape, grid_shape, slot_shape)],
            shape((8, SEQ * BLOCKS), jnp.int32),
        ],
        in_specs=[ANY] * 6,
        out_specs=[VMEM] * 8,
        scratch_shapes=[
            pltpu.VMEM((PICKS, HEADS, SEQ * BLOCKS), jnp.int32),
            pltpu.SMEM((PICKS, HEADS, SEQ * BLOCKS), jnp.int32),
            pltpu.VMEM((1, GLOB), jnp.int32),
            pltpu.SMEM((8, SEQ * BLOCKS), jnp.int32),
            pltpu.VMEM((8, DIM), jnp.int32),
            pltpu.SMEM((8, DIM), jnp.int32),
            *[bf16((TOK, COLS))] * 4,
            bf16((BLOCKS * HEADS, 2 * BLOCK, DIM)),
            bf16(slot_shape),
            bf16(slot_shape),
            bf16(edge_shape),
            *tile_scratch,
            f32((HEADS, TOK, WIDE)),
            f32((HEADS, TOK, WIDE)),
            f32((HEADS, TOK, GLOB)),
            f32((HEADS, TOK, GLOB)),
            bf16((HEADS, TOK, WIDE)),
            bf16((HEADS, TOK, WIDE)),
            bf16((HEADS, TOK, GLOB)),
            bf16((HEADS, TOK, GLOB)),
            bf16((HEADS, TOK, FAR)),
            f32((HEADS, TOK, DIM)),
            f32((HEADS, TOK, DIM)),
            bf16((NPICK + 1, 2 * BLOCK, DIM)),
            bf16(edge_shape),
            *tile_scratch,
            dma((9,)),
            dma((4, 2)),
            dma((4, 2)),
            dma((2,)),
            dma((2, 2)),
            dma((4, 2)),
            dma((2,)),
        ],
        compiler_params=pltpu.CompilerParams(
            collective_id=0, has_side_effects=True, vmem_limit_bytes=48 << 20
        ),
        name="attend",
    )(*operands)
    results = pl.pallas_call(
        collect_kernel,
        out_shape=[narrow] * 4,
        in_specs=[SMEM] + [VMEM] * 8,
        out_specs=[VMEM] * 4,
        scratch_shapes=[f32((BLOCKS * HEADS, 2 * BLOCK, DIM))],
        compiler_params=pltpu.CompilerParams(vmem_limit_bytes=32 << 20),
        name="collect",
    )(table, pos, attended, grad_query, own_key, own_value, edge, tiles, slots)
    return tuple(a.reshape(1, TOK, COLS) for a in results)


def solution(mesh):
    rows = P(None, "seq", "head")
    return jax.shard_map(
        body,
        mesh=mesh,
        in_specs=(rows, rows, rows, rows, P(None, "head", None, None), P()),
        out_specs=(rows, rows, rows, rows),
        check_vma=False,
    )
```

```python
import functools

import jax
import jax.numpy as jnp
from jax import lax
from jax.experimental import pallas as pl
from jax.experimental.pallas import tpu as pltpu
from jax.sharding import PartitionSpec as P

BLOCK = 64
DIM = 128
HEADS = 4
BLOCKS = 4
PICKS = 3
TOK = BLOCK * BLOCKS
COLS = HEADS * DIM
GLOB = 128
TILE = 16
GROUPS = GLOB // TILE
SEQ = 64
RING = 8
NPICK = HEADS * BLOCKS * PICKS
WIDE = (BLOCKS + 2) * BLOCK
FAR = PICKS * BLOCK
SCALE = DIM**-0.5
CHUNKS = (1, 21, 37, 51, SEQ)
EARLY = 9
MINE = 1
BF16 = jnp.bfloat16
F32 = jnp.float32
MESH = pl.DeviceIdType.MESH
VMEM = pl.BlockSpec(memory_space=pltpu.VMEM)
SMEM = pl.BlockSpec(memory_space=pltpu.SMEM)
ANY = pl.BlockSpec(memory_space=pl.ANY)
UPPER, LOWER = pl.ds(0, BLOCK), pl.ds(BLOCK, BLOCK)


def send_to(peer, src, dst, sems):
    return pltpu.make_async_remote_copy(
        src_ref=src,
        dst_ref=dst,
        send_sem=sems.at[0],
        recv_sem=sems.at[1],
        device_id={"seq": peer},
        device_id_type=MESH,
    )


def dot_nt(a, b):
    return lax.dot_general(a, b, (((1,), (1,)), ((), ())), preferred_element_type=F32)


def dot_tn(a, b):
    return lax.dot_general(a, b, (((0,), (0,)), ((), ())), preferred_element_type=F32)


def dot_nn(a, b):
    return jnp.dot(a, b, preferred_element_type=F32)


def named_by(table, device):
    at = device * BLOCKS
    return jnp.maximum(
        jnp.maximum(table[0, at], table[0, at + 1]), jnp.maximum(table[0, at + 2], table[0, at + 3])
    )


class Tiles:
    def __init__(self, me, tiles, part, middle, piece, row, out, sems):
        self.z, self.xc = me // 2 % RING, me // (2 * RING) * 2 + me % 2
        self.tiles, self.part, self.middle, self.piece, self.row, self.out = tiles, part, middle, piece, row, out
        self.sems = sems

    def along_xc(self, k):
        other = lax.rem(self.xc + k, RING)
        return other, (other // 2 * RING + self.z) * 2 + other % 2

    def along_z(self, k):
        other = lax.rem(self.z + k, RING)
        return other, (self.xc // 2 * RING + other) * 2 + self.xc % 2

    def start_first(self):
        for k in range(1, RING):
            other, peer = self.along_xc(k)
            send_to(peer, self.tiles.at[other], self.part.at[self.xc], self.sems.at[0]).start()
        self.part[self.xc] = self.tiles[self.xc]

    def start_second(self):
        rest = pl.ds(0, RING - 1)
        send_to(self.along_xc(1)[1], self.tiles.at[rest], self.part.at[rest], self.sems.at[0]).wait()
        self.middle[...] = jnp.sum(self.part[...].astype(F32), axis=0).astype(BF16)
        for k in range(1, RING):
            other, peer = self.along_z(k)
            send_to(peer, self.middle.at[other], self.piece.at[self.z], self.sems.at[1]).start()
        self.piece[self.z] = self.middle[self.z]

    def start_third(self):
        rest = pl.ds(0, RING - 1)
        send_to(self.along_z(1)[1], self.middle.at[rest], self.piece.at[rest], self.sems.at[1]).wait()
        self.row[self.z] = jnp.sum(self.piece[...].astype(F32), axis=0).astype(BF16)
        for k in range(1, RING):
            _, peer = self.along_z(k)
            send_to(peer, self.row.at[self.z], self.row.at[self.z], self.sems.at[2]).start()

    def start_fourth(self):
        rest = pl.ds(0, RING - 1)
        send_to(self.along_z(1)[1], self.row.at[rest], self.row.at[rest], self.sems.at[2]).wait()
        for k in range(1, RING):
            _, peer = self.along_xc(k)
            send_to(peer, self.row, self.out.at[self.xc], self.sems.at[3]).start()
        self.out[self.xc] = self.row[...]

    def finish(self):
        rest = pl.ds(0, RING - 1)
        send_to(self.along_xc(1)[1], self.tiles.at[rest], self.out.at[rest], self.sems.at[3]).wait()


def main_kernel(
    query_hbm, key_hbm, value_hbm, grad_hbm, rand_hbm, pos_hbm,
    attended, grad_query, own_key, own_value, edge_back, tiles_back, slots_back, table, hot_out,
    rand, rand_smem, pos, table_smem, given_vmem, given_smem, query, key, value, grad, stacked, slots_out, slots, edge, tiles_in, part, middle, piece, row, tiles,
    near_s, near_g, glob_s, glob_g, near_p, near_d, glob_d, glob_p, far_d, row_max, row_sum, picked,
    edge_grads, back_in, back_part, back_middle, back_piece, back_row, back_out,
    local_sems, edge_sems, tile_sems, slot_sems, edge_back_sems, tile_back_sems, slot_back_sems,
):
    me = lax.axis_index("seq")
    right, left = lax.rem(me + 1, SEQ), lax.rem(me + SEQ - 1, SEQ)
    barrier = pltpu.get_barrier_semaphore()
    loads = [
        pltpu.make_async_copy(src, dst, local_sems.at[i])
        for i, (src, dst) in enumerate(
            (
                (rand_hbm, rand),
                (rand_hbm, rand_smem),
                (pos_hbm, pos),
                (key_hbm, key),
                (value_hbm, value),
                (query_hbm, query),
                (grad_hbm, grad),
            )
        )
    ]
    for copy in loads:
        copy.start()

    @pl.loop(1, SEQ)
    def _(k):
        pl.semaphore_signal(barrier, inc=1, device_id={"seq": lax.rem(me + k, SEQ)}, device_id_type=MESH)

    for copy in loads[:5]:
        copy.wait()

    asked = jnp.zeros((HEADS, SEQ * BLOCKS), jnp.int32)
    for p in range(PICKS):
        names = rand[p]
        code = (names & (BLOCKS - 1)) * HEADS + lax.broadcasted_iota(jnp.int32, names.shape, 0)
        asked = jnp.maximum(asked, jnp.where(names >> 2 == me, code, 0))
    asked = jnp.max(asked, axis=0, keepdims=True)
    line = lax.broadcasted_iota(jnp.int32, (8, SEQ * BLOCKS), 0)
    table[...] = jnp.where(line == MINE, me, asked)
    holder = lambda h, j, p: rand_smem[p, h, me * BLOCKS + j] >> 2
    lane = lax.broadcasted_iota(jnp.int32, (8, DIM), 1)
    found = jnp.full((8, DIM), NPICK, jnp.int32)
    for h in range(HEADS):
        for j in range(BLOCKS):
            for p in range(PICKS):
                found = jnp.where(lane == holder(h, j, p), (h * BLOCKS + j) * PICKS + p, found)
    given_vmem[...] = found
    copies = [
        pltpu.make_async_copy(table, table_smem, local_sems.at[7]),
        pltpu.make_async_copy(given_vmem, given_smem, local_sems.at[8]),
    ]
    for copy in copies:
        copy.start()
    given = lambda k: given_smem[0, k]
    want = lambda k: named_by(table_smem, k)

    for j in range(BLOCKS):
        for h in range(HEADS):
            rows, cols = pl.ds(j * BLOCK, BLOCK), pl.ds(h * DIM, DIM)
            stacked[j * HEADS + h, UPPER] = key[rows, cols]
            stacked[j * HEADS + h, LOWER] = value[rows, cols]
    hot = (lax.broadcasted_iota(jnp.int32, (TOK, GLOB), 0) == pos[...] - me * TOK).astype(F32).astype(BF16)
    hot_out[...] = hot
    for c, ref in enumerate((key, value)):
        owned = dot_tn(hot, ref[...]).astype(BF16)
        for g in range(GROUPS):
            for h in range(HEADS):
                tiles_in[g, c * HEADS + h] = owned[g * TILE : (g + 1) * TILE, h * DIM : (h + 1) * DIM]

    for copy in copies:
        copy.wait()

    @pl.loop(0, SEQ)
    def _(k):
        slots_out[k] = stacked[want(k)]

    slots[me] = slots_out[me]

    def send_slots(chunk):
        @pl.loop(CHUNKS[chunk], CHUNKS[chunk + 1])
        def _(k):
            peer = lax.rem(me + k, SEQ)
            send_to(peer, slots_out.at[peer], slots.at[me], slot_sems).start()

    pl.semaphore_wait(barrier, SEQ - 1)
    last, first = pl.ds(TOK - BLOCK, BLOCK), pl.ds(0, BLOCK)
    edges = [
        send_to(left, key.at[first], edge.at[1, UPPER], edge_sems.at[0]),
        send_to(left, value.at[first], edge.at[1, LOWER], edge_sems.at[1]),
        send_to(right, key.at[last], edge.at[0, UPPER], edge_sems.at[2]),
        send_to(right, value.at[last], edge.at[0, LOWER], edge_sems.at[3]),
    ]
    shared = Tiles(me, tiles_in, part, middle, piece, row, tiles, tile_sems)
    shared.start_first()
    for copy in edges:
        copy.start()
    send_slots(0)
    shared.start_second()
    send_slots(1)
    shared.start_third()
    send_slots(2)
    shared.start_fourth()
    send_slots(3)

    loads[5].wait()
    loads[6].wait()
    for copy in edges:
        copy.wait()
    query_block = lax.broadcasted_iota(jnp.int32, (TOK, WIDE), 0) // BLOCK
    key_block = lax.broadcasted_iota(jnp.int32, (TOK, WIDE), 1) // BLOCK
    low = jnp.where(me == 0, 1, 0)
    high = jnp.where(me == SEQ - 1, BLOCKS, BLOCKS + 1)
    offset = key_block - query_block
    band = (offset >= 0) & (offset <= 2) & (key_block >= low) & (key_block <= high)

    def near_keys(cols):
        return jnp.concatenate([edge[0, UPPER, cols], key[:, cols], edge[1, UPPER, cols]], axis=0)

    def near_values(cols):
        return jnp.concatenate([edge[0, LOWER, cols], value[:, cols], edge[1, LOWER, cols]], axis=0)

    def glob_keys(h):
        return jnp.concatenate([tiles[g, h] for g in range(GROUPS)], axis=0)

    def glob_values(h):
        return jnp.concatenate([tiles[g, HEADS + h] for g in range(GROUPS)], axis=0)

    for h in range(HEADS):
        cols = pl.ds(h * DIM, DIM)
        near_s[h] = jnp.where(band, dot_nt(query[:, cols], near_keys(cols)) * SCALE, -1e30)
        near_g[h] = dot_nt(grad[:, cols], near_values(cols))
    shared.finish()
    for h in range(HEADS):
        cols = pl.ds(h * DIM, DIM)
        near, glob = near_s[h], dot_nt(query[:, cols], glob_keys(h)) * SCALE
        top = jnp.maximum(jnp.max(near, axis=1, keepdims=True), jnp.max(glob, axis=1, keepdims=True))
        near, glob = jnp.exp(near - top), jnp.exp(glob - top)
        near_s[h], glob_s[h] = near, glob
        row_max[h] = jnp.broadcast_to(top, (TOK, DIM))
        row_sum[h] = jnp.broadcast_to(
            jnp.sum(near, axis=1, keepdims=True) + jnp.sum(glob, axis=1, keepdims=True), (TOK, DIM)
        )
        glob_g[h] = dot_nt(grad[:, cols], glob_values(h))
    rest = pl.ds(0, SEQ - 1)
    send_to(right, slots_out.at[rest], slots.at[rest], slot_sems).wait()

    block_rows = [slice(j * BLOCK, (j + 1) * BLOCK) for j in range(BLOCKS)]
    picked[NPICK] = jnp.zeros((2 * BLOCK, DIM), BF16)

    def far_keys(h, j):
        return jnp.concatenate([slots[holder(h, j, p), UPPER] for p in range(PICKS)], axis=0)

    for h in range(HEADS):
        cols = pl.ds(h * DIM, DIM)
        q, g = query[:, cols], grad[:, cols]
        keys = [far_keys(h, j) for j in range(BLOCKS)]
        values = [jnp.concatenate([slots[holder(h, j, p), LOWER] for p in range(PICKS)], axis=0) for j in range(BLOCKS)]
        far = jnp.concatenate([dot_nt(q[block_rows[j]], keys[j]) for j in range(BLOCKS)], axis=0) * SCALE
        old_max, old_sum = row_max[h, :, :1], row_sum[h, :, :1]
        new_max = jnp.maximum(old_max, jnp.max(far, axis=1, keepdims=True))
        far = jnp.exp(far - new_max)
        shrink = jnp.exp(old_max - new_max)
        inverse = 1.0 / (old_sum * shrink + jnp.sum(far, axis=1, keepdims=True))
        near, far, glob = near_s[h] * (shrink * inverse), far * inverse, glob_s[h] * (shrink * inverse)
        near_b, far_b, glob_b = near.astype(BF16), far.astype(BF16), glob.astype(BF16)
        mixed = dot_nn(near_b, near_values(cols)) + dot_nn(glob_b, glob_values(h))
        mixed += jnp.concatenate([dot_nn(far_b[block_rows[j]], values[j]) for j in range(BLOCKS)], axis=0)
        attended[:, cols] = mixed.astype(BF16)
        delta = jnp.sum(g.astype(F32) * mixed, axis=1, keepdims=True)
        far_g = jnp.concatenate([dot_nt(g[block_rows[j]], values[j]) for j in range(BLOCKS)], axis=0)
        far_change = (far * (far_g - delta)).astype(BF16)
        far_d[h] = far_change
        for j in range(BLOCKS):
            far_key = (dot_tn(far_change[block_rows[j]], q[block_rows[j]]) * SCALE).astype(BF16)
            far_value = dot_tn(far_b[block_rows[j]], g[block_rows[j]]).astype(BF16)
            for p in range(PICKS):
                at = (h * BLOCKS + j) * PICKS + p
                picked[at, UPPER] = far_key[p * BLOCK : (p + 1) * BLOCK]
                picked[at, LOWER] = far_value[p * BLOCK : (p + 1) * BLOCK]
        near_p[h] = near_b
        glob_p[h] = glob_b
        near_d[h] = (near * (near_g[h] - delta)).astype(BF16)
        glob_d[h] = (glob * (glob_g[h] - delta)).astype(BF16)

    def return_slots(begin, end):
        @pl.loop(begin, end)
        def _(k):
            peer = lax.rem(me + k, SEQ)
            slots_out[peer] = picked[given(peer)]
            send_to(peer, slots_out.at[peer], slots_back.at[me], slot_back_sems).start()

    return_slots(CHUNKS[0], EARLY)
    for h in range(HEADS):
        cols = pl.ds(h * DIM, DIM)
        glob_key = (dot_tn(glob_d[h], query[:, cols]) * SCALE).astype(BF16)
        glob_value = dot_tn(glob_p[h], grad[:, cols]).astype(BF16)
        for g in range(GROUPS):
            back_in[g, h] = glob_key[g * TILE : (g + 1) * TILE]
            back_in[g, HEADS + h] = glob_value[g * TILE : (g + 1) * TILE]
    summed = Tiles(me, back_in, back_part, back_middle, back_piece, back_row, back_out, tile_back_sems)
    summed.start_first()
    return_slots(EARLY, CHUNKS[1])
    slots_back[me] = picked[given(me)]
    for h in range(HEADS):
        cols = pl.ds(h * DIM, DIM)
        q, g = query[:, cols], grad[:, cols]
        near_key = dot_tn(near_d[h], q) * SCALE
        near_value = dot_tn(near_p[h], g)
        own_key[:, cols] = near_key[BLOCK : BLOCK + TOK]
        own_value[:, cols] = near_value[BLOCK : BLOCK + TOK]
        edge_grads[0, UPPER, cols] = near_key[:BLOCK].astype(BF16)
        edge_grads[0, LOWER, cols] = near_value[:BLOCK].astype(BF16)
        edge_grads[1, UPPER, cols] = near_key[BLOCK + TOK :].astype(BF16)
        edge_grads[1, LOWER, cols] = near_value[BLOCK + TOK :].astype(BF16)
    edges = [
        send_to(left, edge_grads.at[0], edge_back.at[1], edge_back_sems.at[0]),
        send_to(right, edge_grads.at[1], edge_back.at[0], edge_back_sems.at[1]),
    ]
    for copy in edges:
        copy.start()
    summed.start_second()
    return_slots(CHUNKS[1], CHUNKS[2])
    summed.start_third()
    return_slots(CHUNKS[2], CHUNKS[3])
    summed.start_fourth()
    return_slots(CHUNKS[3], CHUNKS[4])
    for h in range(HEADS):
        cols = pl.ds(h * DIM, DIM)
        change = dot_nn(near_d[h], near_keys(cols)) + dot_nn(glob_d[h], glob_keys(h))
        change += jnp.concatenate([dot_nn(far_d[h, block_rows[j]], far_keys(h, j)) for j in range(BLOCKS)], axis=0)
        grad_query[:, cols] = (change * SCALE).astype(BF16)
    summed.finish()
    tiles_back[...] = back_out[...]
    for copy in edges:
        copy.wait()
    send_to(right, slots_out.at[rest], slots_back.at[rest], slot_back_sems).wait()


def collect_kernel(
    table, hot, attended_in, query_in, own_key, own_value, edge, tiles, slots,
    attended, grad_query, grad_key, grad_value, total,
):
    me = table[MINE, 0]
    attended[...] = attended_in[...]
    grad_query[...] = query_in[...]
    for j in range(BLOCKS):
        for h in range(HEADS):
            rows, cols = pl.ds(j * BLOCK, BLOCK), pl.ds(h * DIM, DIM)
            total[j * HEADS + h, UPPER] = own_key[rows, cols]
            total[j * HEADS + h, LOWER] = own_value[rows, cols]

    @pl.loop(0, SEQ)
    def _(k):
        total[named_by(table, k)] += slots[k].astype(F32)

    from_left = jnp.where(me == 0, 0.0, 1.0)
    from_right = jnp.where(me == SEQ - 1, 0.0, 1.0)
    for h in range(HEADS):
        cols = pl.ds(h * DIM, DIM)
        for c, out in enumerate((grad_key, grad_value)):
            part = pl.ds(c * BLOCK, BLOCK)
            glob = jnp.concatenate([tiles[g, c * HEADS + h] for g in range(GROUPS)], axis=0)
            placed = dot_nn(hot[...], glob)
            for j in range(BLOCKS):
                whole = total[j * HEADS + h, part] + placed[j * BLOCK : (j + 1) * BLOCK]
                if j == 0:
                    whole += edge[0, part, cols].astype(F32) * from_left
                if j == BLOCKS - 1:
                    whole += edge[1, part, cols].astype(F32) * from_right
                out[pl.ds(j * BLOCK, BLOCK), cols] = whole.astype(BF16)


def body(query_rows, key_rows, value_rows, grad_out, rand_blocks, global_pos):
    arrays = [a.reshape(TOK, COLS) for a in (query_rows, key_rows, value_rows, grad_out)]
    names = rand_blocks.transpose(0, 3, 1, 2).reshape(PICKS, HEADS, SEQ * BLOCKS)
    pos = global_pos[None, :]
    operands = [pltpu.with_memory_space_constraint(a, pltpu.HBM) for a in (*arrays, names, pos)]
    shape = jax.ShapeDtypeStruct
    slot_shape, edge_shape = (SEQ, 2 * BLOCK, DIM), (2, 2 * BLOCK, COLS)
    grid_shape, row_shape = (RING, RING, TILE, DIM), (RING, TILE, DIM)
    wide, narrow = shape((TOK, COLS), F32), shape((TOK, COLS), BF16)
    bf16 = lambda dims: pltpu.VMEM(dims, BF16)
    f32 = lambda dims: pltpu.VMEM(dims, F32)
    dma = pltpu.SemaphoreType.DMA
    tile_scratch = [bf16(grid_shape), bf16(grid_shape), bf16(row_shape), bf16(row_shape), bf16(row_shape), bf16(grid_shape)]
    attended, grad_query, own_key, own_value, edge, tiles, slots, table, hot = pl.pallas_call(
        main_kernel,
        out_shape=[
            *[narrow, narrow, wide, wide],
            *[shape(dims, BF16) for dims in (edge_shape, grid_shape, slot_shape)],
            shape((8, SEQ * BLOCKS), jnp.int32),
            shape((TOK, GLOB), BF16),
        ],
        in_specs=[ANY] * 6,
        out_specs=[VMEM] * 9,
        scratch_shapes=[
            pltpu.VMEM((PICKS, HEADS, SEQ * BLOCKS), jnp.int32),
            pltpu.SMEM((PICKS, HEADS, SEQ * BLOCKS), jnp.int32),
            pltpu.VMEM((1, GLOB), jnp.int32),
            pltpu.SMEM((8, SEQ * BLOCKS), jnp.int32),
            pltpu.VMEM((8, DIM), jnp.int32),
            pltpu.SMEM((8, DIM), jnp.int32),
            *[bf16((TOK, COLS))] * 4,
            bf16((BLOCKS * HEADS, 2 * BLOCK, DIM)),
            bf16(slot_shape),
            bf16(slot_shape),
            bf16(edge_shape),
            *tile_scratch,
            f32((HEADS, TOK, WIDE)),
            f32((HEADS, TOK, WIDE)),
            f32((HEADS, TOK, GLOB)),
            f32((HEADS, TOK, GLOB)),
            bf16((HEADS, TOK, WIDE)),
            bf16((HEADS, TOK, WIDE)),
            bf16((HEADS, TOK, GLOB)),
            bf16((HEADS, TOK, GLOB)),
            bf16((HEADS, TOK, FAR)),
            f32((HEADS, TOK, DIM)),
            f32((HEADS, TOK, DIM)),
            bf16((NPICK + 1, 2 * BLOCK, DIM)),
            bf16(edge_shape),
            *tile_scratch,
            dma((9,)),
            dma((4, 2)),
            dma((4, 2)),
            dma((2,)),
            dma((2, 2)),
            dma((4, 2)),
            dma((2,)),
        ],
        compiler_params=pltpu.CompilerParams(
            collective_id=0, has_side_effects=True, vmem_limit_bytes=48 << 20
        ),
        name="attend",
    )(*operands)
    results = pl.pallas_call(
        collect_kernel,
        out_shape=[narrow] * 4,
        in_specs=[SMEM] + [VMEM] * 8,
        out_specs=[VMEM] * 4,
        scratch_shapes=[f32((BLOCKS * HEADS, 2 * BLOCK, DIM))],
        compiler_params=pltpu.CompilerParams(vmem_limit_bytes=32 << 20),
        name="collect",
    )(table, hot, attended, grad_query, own_key, own_value, edge, tiles, slots)
    return tuple(a.reshape(1, TOK, COLS) for a in results)


def solution(mesh):
    rows = P(None, "seq", "head")
    return jax.shard_map(
        body,
        mesh=mesh,
        in_specs=(rows, rows, rows, rows, P(None, "head", None, None), P()),
        out_specs=(rows, rows, rows, rows),
        check_vma=False,
    )
```

```python
import functools

import jax
import jax.numpy as jnp
from jax import lax
from jax.experimental import pallas as pl
from jax.experimental.pallas import tpu as pltpu
from jax.sharding import PartitionSpec as P

BLOCK = 64
DIM = 128
HEADS = 4
BLOCKS = 4
PICKS = 3
TOK = BLOCK * BLOCKS
COLS = HEADS * DIM
GLOB = 128
TILE = 16
GROUPS = GLOB // TILE
SEQ = 64
RING = 8
NPICK = HEADS * BLOCKS * PICKS
WIDE = (BLOCKS + 2) * BLOCK
FAR = PICKS * BLOCK
SCALE = DIM**-0.5
CHUNKS = (1, 21, 37, 51, SEQ)
EARLY = 9
MINE = 1
BF16 = jnp.bfloat16
F32 = jnp.float32
MESH = pl.DeviceIdType.MESH
VMEM = pl.BlockSpec(memory_space=pltpu.VMEM)
SMEM = pl.BlockSpec(memory_space=pltpu.SMEM)
ANY = pl.BlockSpec(memory_space=pl.ANY)
UPPER, LOWER = pl.ds(0, BLOCK), pl.ds(BLOCK, BLOCK)


def send_to(peer, src, dst, sems):
    return pltpu.make_async_remote_copy(
        src_ref=src,
        dst_ref=dst,
        send_sem=sems.at[0],
        recv_sem=sems.at[1],
        device_id={"seq": peer},
        device_id_type=MESH,
    )


def dot_nt(a, b):
    return lax.dot_general(a, b, (((1,), (1,)), ((), ())), preferred_element_type=F32)


def dot_tn(a, b):
    return lax.dot_general(a, b, (((0,), (0,)), ((), ())), preferred_element_type=F32)


def dot_nn(a, b):
    return jnp.dot(a, b, preferred_element_type=F32)


def named_by(table, device):
    at = device * BLOCKS
    return jnp.maximum(
        jnp.maximum(table[0, at], table[0, at + 1]), jnp.maximum(table[0, at + 2], table[0, at + 3])
    )


class Tiles:
    def __init__(self, me, tiles, part, middle, piece, row, out, sems):
        self.z, self.xc = me // 2 % RING, me // (2 * RING) * 2 + me % 2
        self.tiles, self.part, self.middle, self.piece, self.row, self.out = tiles, part, middle, piece, row, out
        self.sems = sems

    def along_xc(self, k):
        other = lax.rem(self.xc + k, RING)
        return other, (other // 2 * RING + self.z) * 2 + other % 2

    def along_z(self, k):
        other = lax.rem(self.z + k, RING)
        return other, (self.xc // 2 * RING + other) * 2 + self.xc % 2

    def start_first(self):
        for k in range(1, RING):
            other, peer = self.along_xc(k)
            send_to(peer, self.tiles.at[other], self.part.at[self.xc], self.sems.at[0]).start()
        self.part[self.xc] = self.tiles[self.xc]

    def start_second(self):
        rest = pl.ds(0, RING - 1)
        send_to(self.along_xc(1)[1], self.tiles.at[rest], self.part.at[rest], self.sems.at[0]).wait()
        self.middle[...] = jnp.sum(self.part[...].astype(F32), axis=0).astype(BF16)
        for k in range(1, RING):
            other, peer = self.along_z(k)
            send_to(peer, self.middle.at[other], self.piece.at[self.z], self.sems.at[1]).start()
        self.piece[self.z] = self.middle[self.z]

    def start_third(self):
        rest = pl.ds(0, RING - 1)
        send_to(self.along_z(1)[1], self.middle.at[rest], self.piece.at[rest], self.sems.at[1]).wait()
        self.row[self.z] = jnp.sum(self.piece[...].astype(F32), axis=0).astype(BF16)
        for k in range(1, RING):
            _, peer = self.along_z(k)
            send_to(peer, self.row.at[self.z], self.row.at[self.z], self.sems.at[2]).start()

    def start_fourth(self):
        rest = pl.ds(0, RING - 1)
        send_to(self.along_z(1)[1], self.row.at[rest], self.row.at[rest], self.sems.at[2]).wait()
        for k in range(1, RING):
            _, peer = self.along_xc(k)
            send_to(peer, self.row, self.out.at[self.xc], self.sems.at[3]).start()
        self.out[self.xc] = self.row[...]

    def finish(self):
        rest = pl.ds(0, RING - 1)
        send_to(self.along_xc(1)[1], self.tiles.at[rest], self.out.at[rest], self.sems.at[3]).wait()


def main_kernel(
    query_hbm, key_hbm, value_hbm, grad_hbm, rand_hbm, pos_hbm,
    attended, grad_query, own, edge_back, tiles_back, slots_back, table, hot_out,
    rand, rand_smem, pos, table_smem, given_vmem, given_smem, query, key, value, grad, stacked, slots_out, slots, edge, tiles_in, part, middle, piece, row, tiles,
    near_s, near_g, glob_s, glob_g, near_p, near_d, glob_d, glob_p, far_d, row_max, row_sum, picked,
    edge_grads, back_in, back_part, back_middle, back_piece, back_row, back_out,
    local_sems, edge_sems, tile_sems, slot_sems, edge_back_sems, tile_back_sems, slot_back_sems,
):
    me = lax.axis_index("seq")
    right, left = lax.rem(me + 1, SEQ), lax.rem(me + SEQ - 1, SEQ)
    barrier = pltpu.get_barrier_semaphore()
    loads = [
        pltpu.make_async_copy(src, dst, local_sems.at[i])
        for i, (src, dst) in enumerate(
            (
                (rand_hbm, rand),
                (rand_hbm, rand_smem),
                (pos_hbm, pos),
                (key_hbm, key),
                (value_hbm, value),
                (query_hbm, query),
                (grad_hbm, grad),
            )
        )
    ]
    for copy in loads:
        copy.start()

    @pl.loop(1, SEQ)
    def _(k):
        pl.semaphore_signal(barrier, inc=1, device_id={"seq": lax.rem(me + k, SEQ)}, device_id_type=MESH)

    for copy in loads[:5]:
        copy.wait()

    asked = jnp.zeros((HEADS, SEQ * BLOCKS), jnp.int32)
    for p in range(PICKS):
        names = rand[p]
        code = (names & (BLOCKS - 1)) * HEADS + lax.broadcasted_iota(jnp.int32, names.shape, 0)
        asked = jnp.maximum(asked, jnp.where(names >> 2 == me, code, 0))
    asked = jnp.max(asked, axis=0, keepdims=True)
    line = lax.broadcasted_iota(jnp.int32, (8, SEQ * BLOCKS), 0)
    table[...] = jnp.where(line == MINE, me, asked)
    holder = lambda h, j, p: rand_smem[p, h, me * BLOCKS + j] >> 2
    lane = lax.broadcasted_iota(jnp.int32, (8, DIM), 1)
    found = jnp.full((8, DIM), NPICK, jnp.int32)
    for h in range(HEADS):
        for j in range(BLOCKS):
            for p in range(PICKS):
                found = jnp.where(lane == holder(h, j, p), (h * BLOCKS + j) * PICKS + p, found)
    given_vmem[...] = found
    copies = [
        pltpu.make_async_copy(table, table_smem, local_sems.at[7]),
        pltpu.make_async_copy(given_vmem, given_smem, local_sems.at[8]),
    ]
    for copy in copies:
        copy.start()
    given = lambda k: given_smem[0, k]
    want = lambda k: named_by(table_smem, k)

    for j in range(BLOCKS):
        for h in range(HEADS):
            rows, cols = pl.ds(j * BLOCK, BLOCK), pl.ds(h * DIM, DIM)
            stacked[j * HEADS + h, UPPER] = key[rows, cols]
            stacked[j * HEADS + h, LOWER] = value[rows, cols]
    hot = (lax.broadcasted_iota(jnp.int32, (TOK, GLOB), 0) == pos[...] - me * TOK).astype(F32).astype(BF16)
    hot_out[...] = hot
    for c, ref in enumerate((key, value)):
        owned = dot_tn(hot, ref[...]).astype(BF16)
        for g in range(GROUPS):
            for h in range(HEADS):
                tiles_in[g, c * HEADS + h] = owned[g * TILE : (g + 1) * TILE, h * DIM : (h + 1) * DIM]

    for copy in copies:
        copy.wait()

    @pl.loop(0, SEQ)
    def _(k):
        slots_out[k] = stacked[want(k)]

    slots[me] = slots_out[me]

    def send_slots(chunk):
        @pl.loop(CHUNKS[chunk], CHUNKS[chunk + 1])
        def _(k):
            peer = lax.rem(me + k, SEQ)
            send_to(peer, slots_out.at[peer], slots.at[me], slot_sems).start()

    pl.semaphore_wait(barrier, SEQ - 1)
    last, first = pl.ds(TOK - BLOCK, BLOCK), pl.ds(0, BLOCK)
    edges = [
        send_to(left, key.at[first], edge.at[1, UPPER], edge_sems.at[0]),
        send_to(left, value.at[first], edge.at[1, LOWER], edge_sems.at[1]),
        send_to(right, key.at[last], edge.at[0, UPPER], edge_sems.at[2]),
        send_to(right, value.at[last], edge.at[0, LOWER], edge_sems.at[3]),
    ]
    shared = Tiles(me, tiles_in, part, middle, piece, row, tiles, tile_sems)
    shared.start_first()
    for copy in edges:
        copy.start()
    send_slots(0)
    shared.start_second()
    send_slots(1)
    shared.start_third()
    send_slots(2)
    shared.start_fourth()
    send_slots(3)

    loads[5].wait()
    loads[6].wait()
    for copy in edges:
        copy.wait()
    query_block = lax.broadcasted_iota(jnp.int32, (TOK, WIDE), 0) // BLOCK
    key_block = lax.broadcasted_iota(jnp.int32, (TOK, WIDE), 1) // BLOCK
    low = jnp.where(me == 0, 1, 0)
    high = jnp.where(me == SEQ - 1, BLOCKS, BLOCKS + 1)
    offset = key_block - query_block
    band = (offset >= 0) & (offset <= 2) & (key_block >= low) & (key_block <= high)

    def near_keys(cols):
        return jnp.concatenate([edge[0, UPPER, cols], key[:, cols], edge[1, UPPER, cols]], axis=0)

    def near_values(cols):
        return jnp.concatenate([edge[0, LOWER, cols], value[:, cols], edge[1, LOWER, cols]], axis=0)

    def glob_keys(h):
        return jnp.concatenate([tiles[g, h] for g in range(GROUPS)], axis=0)

    def glob_values(h):
        return jnp.concatenate([tiles[g, HEADS + h] for g in range(GROUPS)], axis=0)

    for h in range(HEADS):
        cols = pl.ds(h * DIM, DIM)
        near_s[h] = jnp.where(band, dot_nt(query[:, cols], near_keys(cols)) * SCALE, -1e30)
        near_g[h] = dot_nt(grad[:, cols], near_values(cols))
    shared.finish()
    for h in range(HEADS):
        cols = pl.ds(h * DIM, DIM)
        near, glob = near_s[h], dot_nt(query[:, cols], glob_keys(h)) * SCALE
        top = jnp.maximum(jnp.max(near, axis=1, keepdims=True), jnp.max(glob, axis=1, keepdims=True))
        near, glob = jnp.exp(near - top), jnp.exp(glob - top)
        near_s[h], glob_s[h] = near, glob
        row_max[h] = jnp.broadcast_to(top, (TOK, DIM))
        row_sum[h] = jnp.broadcast_to(
            jnp.sum(near, axis=1, keepdims=True) + jnp.sum(glob, axis=1, keepdims=True), (TOK, DIM)
        )
        glob_g[h] = dot_nt(grad[:, cols], glob_values(h))
    rest = pl.ds(0, SEQ - 1)
    send_to(right, slots_out.at[rest], slots.at[rest], slot_sems).wait()

    block_rows = [slice(j * BLOCK, (j + 1) * BLOCK) for j in range(BLOCKS)]
    picked[NPICK] = jnp.zeros((2 * BLOCK, DIM), BF16)

    def far_keys(h, j):
        return jnp.concatenate([slots[holder(h, j, p), UPPER] for p in range(PICKS)], axis=0)

    for h in range(HEADS):
        cols = pl.ds(h * DIM, DIM)
        q, g = query[:, cols], grad[:, cols]
        keys = [far_keys(h, j) for j in range(BLOCKS)]
        values = [jnp.concatenate([slots[holder(h, j, p), LOWER] for p in range(PICKS)], axis=0) for j in range(BLOCKS)]
        far = jnp.concatenate([dot_nt(q[block_rows[j]], keys[j]) for j in range(BLOCKS)], axis=0) * SCALE
        old_max, old_sum = row_max[h, :, :1], row_sum[h, :, :1]
        new_max = jnp.maximum(old_max, jnp.max(far, axis=1, keepdims=True))
        far = jnp.exp(far - new_max)
        shrink = jnp.exp(old_max - new_max)
        inverse = 1.0 / (old_sum * shrink + jnp.sum(far, axis=1, keepdims=True))
        near, far, glob = near_s[h] * (shrink * inverse), far * inverse, glob_s[h] * (shrink * inverse)
        near_b, far_b, glob_b = near.astype(BF16), far.astype(BF16), glob.astype(BF16)
        mixed = dot_nn(near_b, near_values(cols)) + dot_nn(glob_b, glob_values(h))
        mixed += jnp.concatenate([dot_nn(far_b[block_rows[j]], values[j]) for j in range(BLOCKS)], axis=0)
        attended[:, cols] = mixed.astype(BF16)
        delta = jnp.sum(g.astype(F32) * mixed, axis=1, keepdims=True)
        far_g = jnp.concatenate([dot_nt(g[block_rows[j]], values[j]) for j in range(BLOCKS)], axis=0)
        far_change = (far * (far_g - delta)).astype(BF16)
        far_d[h] = far_change
        for j in range(BLOCKS):
            far_key = (dot_tn(far_change[block_rows[j]], q[block_rows[j]]) * SCALE).astype(BF16)
            far_value = dot_tn(far_b[block_rows[j]], g[block_rows[j]]).astype(BF16)
            for p in range(PICKS):
                at = (h * BLOCKS + j) * PICKS + p
                picked[at, UPPER] = far_key[p * BLOCK : (p + 1) * BLOCK]
                picked[at, LOWER] = far_value[p * BLOCK : (p + 1) * BLOCK]
        near_p[h] = near_b
        glob_p[h] = glob_b
        near_d[h] = (near * (near_g[h] - delta)).astype(BF16)
        glob_d[h] = (glob * (glob_g[h] - delta)).astype(BF16)

    def return_slots(begin, end):
        @pl.loop(begin, end)
        def _(k):
            peer = lax.rem(me + k, SEQ)
            slots_out[peer] = picked[given(peer)]
            send_to(peer, slots_out.at[peer], slots_back.at[me], slot_back_sems).start()

    return_slots(CHUNKS[0], EARLY)
    for h in range(HEADS):
        cols = pl.ds(h * DIM, DIM)
        glob_key = (dot_tn(glob_d[h], query[:, cols]) * SCALE).astype(BF16)
        glob_value = dot_tn(glob_p[h], grad[:, cols]).astype(BF16)
        for g in range(GROUPS):
            back_in[g, h] = glob_key[g * TILE : (g + 1) * TILE]
            back_in[g, HEADS + h] = glob_value[g * TILE : (g + 1) * TILE]
    summed = Tiles(me, back_in, back_part, back_middle, back_piece, back_row, back_out, tile_back_sems)
    summed.start_first()
    return_slots(EARLY, CHUNKS[1])
    slots_back[me] = picked[given(me)]
    for h in range(HEADS):
        cols = pl.ds(h * DIM, DIM)
        q, g = query[:, cols], grad[:, cols]
        near_key = dot_tn(near_d[h], q) * SCALE
        near_value = dot_tn(near_p[h], g)
        for j in range(BLOCKS):
            own[j * HEADS + h, UPPER] = near_key[(j + 1) * BLOCK : (j + 2) * BLOCK]
            own[j * HEADS + h, LOWER] = near_value[(j + 1) * BLOCK : (j + 2) * BLOCK]
        edge_grads[0, UPPER, cols] = near_key[:BLOCK].astype(BF16)
        edge_grads[0, LOWER, cols] = near_value[:BLOCK].astype(BF16)
        edge_grads[1, UPPER, cols] = near_key[BLOCK + TOK :].astype(BF16)
        edge_grads[1, LOWER, cols] = near_value[BLOCK + TOK :].astype(BF16)
    edges = [
        send_to(left, edge_grads.at[0], edge_back.at[1], edge_back_sems.at[0]),
        send_to(right, edge_grads.at[1], edge_back.at[0], edge_back_sems.at[1]),
    ]
    for copy in edges:
        copy.start()
    summed.start_second()
    return_slots(CHUNKS[1], CHUNKS[2])
    summed.start_third()
    return_slots(CHUNKS[2], CHUNKS[3])
    summed.start_fourth()
    return_slots(CHUNKS[3], CHUNKS[4])
    for h in range(HEADS):
        cols = pl.ds(h * DIM, DIM)
        change = dot_nn(near_d[h], near_keys(cols)) + dot_nn(glob_d[h], glob_keys(h))
        change += jnp.concatenate([dot_nn(far_d[h, block_rows[j]], far_keys(h, j)) for j in range(BLOCKS)], axis=0)
        grad_query[:, cols] = (change * SCALE).astype(BF16)
    summed.finish()
    tiles_back[...] = back_out[...]
    for copy in edges:
        copy.wait()
    send_to(right, slots_out.at[rest], slots_back.at[rest], slot_back_sems).wait()


def collect_kernel(
    table, hot, attended_in, query_in, own, edge, tiles, slots,
    attended, grad_query, grad_key, grad_value, total, sems,
):
    me = table[MINE, 0]
    passed = [
        pltpu.make_async_copy(attended_in, attended, sems.at[0]),
        pltpu.make_async_copy(query_in, grad_query, sems.at[1]),
    ]
    for copy in passed:
        copy.start()
    total[...] = own[...]

    @pl.loop(0, SEQ)
    def _(k):
        total[named_by(table, k)] += slots[k].astype(F32)

    from_left = jnp.where(me == 0, 0.0, 1.0)
    from_right = jnp.where(me == SEQ - 1, 0.0, 1.0)
    for h in range(HEADS):
        cols = pl.ds(h * DIM, DIM)
        for c, out in enumerate((grad_key, grad_value)):
            part = pl.ds(c * BLOCK, BLOCK)
            glob = jnp.concatenate([tiles[g, c * HEADS + h] for g in range(GROUPS)], axis=0)
            placed = dot_nn(hot[...], glob)
            for j in range(BLOCKS):
                whole = total[j * HEADS + h, part] + placed[j * BLOCK : (j + 1) * BLOCK]
                if j == 0:
                    whole += edge[0, part, cols].astype(F32) * from_left
                if j == BLOCKS - 1:
                    whole += edge[1, part, cols].astype(F32) * from_right
                out[pl.ds(j * BLOCK, BLOCK), cols] = whole.astype(BF16)
    for copy in passed:
        copy.wait()


def body(query_rows, key_rows, value_rows, grad_out, rand_blocks, global_pos):
    arrays = [a.reshape(TOK, COLS) for a in (query_rows, key_rows, value_rows, grad_out)]
    names = rand_blocks.transpose(0, 3, 1, 2).reshape(PICKS, HEADS, SEQ * BLOCKS)
    pos = global_pos[None, :]
    operands = [pltpu.with_memory_space_constraint(a, pltpu.HBM) for a in (*arrays, names, pos)]
    shape = jax.ShapeDtypeStruct
    slot_shape, edge_shape = (SEQ, 2 * BLOCK, DIM), (2, 2 * BLOCK, COLS)
    grid_shape, row_shape = (RING, RING, TILE, DIM), (RING, TILE, DIM)
    own_shape, narrow = shape((BLOCKS * HEADS, 2 * BLOCK, DIM), F32), shape((TOK, COLS), BF16)
    bf16 = lambda dims: pltpu.VMEM(dims, BF16)
    f32 = lambda dims: pltpu.VMEM(dims, F32)
    dma = pltpu.SemaphoreType.DMA
    tile_scratch = [bf16(grid_shape), bf16(grid_shape), bf16(row_shape), bf16(row_shape), bf16(row_shape), bf16(grid_shape)]
    attended, grad_query, own, edge, tiles, slots, table, hot = pl.pallas_call(
        main_kernel,
        out_shape=[
            *[narrow, narrow, own_shape],
            *[shape(dims, BF16) for dims in (edge_shape, grid_shape, slot_shape)],
            shape((8, SEQ * BLOCKS), jnp.int32),
            shape((TOK, GLOB), BF16),
        ],
        in_specs=[ANY] * 6,
        out_specs=[VMEM] * 8,
        scratch_shapes=[
            pltpu.VMEM((PICKS, HEADS, SEQ * BLOCKS), jnp.int32),
            pltpu.SMEM((PICKS, HEADS, SEQ * BLOCKS), jnp.int32),
            pltpu.VMEM((1, GLOB), jnp.int32),
            pltpu.SMEM((8, SEQ * BLOCKS), jnp.int32),
            pltpu.VMEM((8, DIM), jnp.int32),
            pltpu.SMEM((8, DIM), jnp.int32),
            *[bf16((TOK, COLS))] * 4,
            bf16((BLOCKS * HEADS, 2 * BLOCK, DIM)),
            bf16(slot_shape),
            bf16(slot_shape),
            bf16(edge_shape),
            *tile_scratch,
            f32((HEADS, TOK, WIDE)),
            f32((HEADS, TOK, WIDE)),
            f32((HEADS, TOK, GLOB)),
            f32((HEADS, TOK, GLOB)),
            bf16((HEADS, TOK, WIDE)),
            bf16((HEADS, TOK, WIDE)),
            bf16((HEADS, TOK, GLOB)),
            bf16((HEADS, TOK, GLOB)),
            bf16((HEADS, TOK, FAR)),
            f32((HEADS, TOK, DIM)),
            f32((HEADS, TOK, DIM)),
            bf16((NPICK + 1, 2 * BLOCK, DIM)),
            bf16(edge_shape),
            *tile_scratch,
            dma((9,)),
            dma((4, 2)),
            dma((4, 2)),
            dma((2,)),
            dma((2, 2)),
            dma((4, 2)),
            dma((2,)),
        ],
        compiler_params=pltpu.CompilerParams(
            collective_id=0, has_side_effects=True, vmem_limit_bytes=48 << 20
        ),
        name="attend",
    )(*operands)
    results = pl.pallas_call(
        collect_kernel,
        out_shape=[narrow] * 4,
        in_specs=[SMEM] + [VMEM] * 7,
        out_specs=[ANY, ANY, VMEM, VMEM],
        scratch_shapes=[f32((BLOCKS * HEADS, 2 * BLOCK, DIM)), dma((2,))],
        compiler_params=pltpu.CompilerParams(vmem_limit_bytes=32 << 20),
        name="collect",
    )(table, hot, attended, grad_query, own, edge, tiles, slots)
    return tuple(a.reshape(1, TOK, COLS) for a in results)


def solution(mesh):
    rows = P(None, "seq", "head")
    return jax.shard_map(
        body,
        mesh=mesh,
        in_specs=(rows, rows, rows, rows, P(None, "head", None, None), P()),
        out_specs=(rows, rows, rows, rows),
        check_vma=False,
    )
```

```python
import functools

import jax
import jax.numpy as jnp
from jax import lax
from jax.experimental import pallas as pl
from jax.experimental.pallas import tpu as pltpu
from jax.sharding import PartitionSpec as P

BLOCK = 64
DIM = 128
HEADS = 4
BLOCKS = 4
PICKS = 3
TOK = BLOCK * BLOCKS
COLS = HEADS * DIM
GLOB = 128
TILE = 16
GROUPS = GLOB // TILE
SEQ = 64
RING = 8
NPICK = HEADS * BLOCKS * PICKS
WIDE = (BLOCKS + 2) * BLOCK
FAR = PICKS * BLOCK
SCALE = DIM**-0.5
CHUNKS = (1, 21, 37, 51, SEQ)
EARLY = 9
MINE = 1
BF16 = jnp.bfloat16
F32 = jnp.float32
MESH = pl.DeviceIdType.MESH
VMEM = pl.BlockSpec(memory_space=pltpu.VMEM)
SMEM = pl.BlockSpec(memory_space=pltpu.SMEM)
ANY = pl.BlockSpec(memory_space=pl.ANY)
UPPER, LOWER = pl.ds(0, BLOCK), pl.ds(BLOCK, BLOCK)


def send_to(peer, src, dst, sems):
    return pltpu.make_async_remote_copy(
        src_ref=src,
        dst_ref=dst,
        send_sem=sems.at[0],
        recv_sem=sems.at[1],
        device_id={"seq": peer},
        device_id_type=MESH,
    )


def dot_nt(a, b):
    return lax.dot_general(a, b, (((1,), (1,)), ((), ())), preferred_element_type=F32)


def dot_tn(a, b):
    return lax.dot_general(a, b, (((0,), (0,)), ((), ())), preferred_element_type=F32)


def dot_nn(a, b):
    return jnp.dot(a, b, preferred_element_type=F32)


def named_by(table, device):
    at = device * BLOCKS
    return jnp.maximum(
        jnp.maximum(table[0, at], table[0, at + 1]), jnp.maximum(table[0, at + 2], table[0, at + 3])
    )


class Tiles:
    def __init__(self, me, tiles, part, middle, piece, row, out, sems):
        self.z, self.xc = me // 2 % RING, me // (2 * RING) * 2 + me % 2
        self.tiles, self.part, self.middle, self.piece, self.row, self.out = tiles, part, middle, piece, row, out
        self.sems = sems

    def along_xc(self, k):
        other = lax.rem(self.xc + k, RING)
        return other, (other // 2 * RING + self.z) * 2 + other % 2

    def along_z(self, k):
        other = lax.rem(self.z + k, RING)
        return other, (self.xc // 2 * RING + other) * 2 + self.xc % 2

    def start_first(self):
        for k in range(1, RING):
            other, peer = self.along_xc(k)
            send_to(peer, self.tiles.at[other], self.part.at[self.xc], self.sems.at[0]).start()
        self.part[self.xc] = self.tiles[self.xc]

    def start_second(self):
        rest = pl.ds(0, RING - 1)
        send_to(self.along_xc(1)[1], self.tiles.at[rest], self.part.at[rest], self.sems.at[0]).wait()
        self.middle[...] = jnp.sum(self.part[...].astype(F32), axis=0).astype(BF16)
        for k in range(1, RING):
            other, peer = self.along_z(k)
            send_to(peer, self.middle.at[other], self.piece.at[self.z], self.sems.at[1]).start()
        self.piece[self.z] = self.middle[self.z]

    def start_third(self):
        rest = pl.ds(0, RING - 1)
        send_to(self.along_z(1)[1], self.middle.at[rest], self.piece.at[rest], self.sems.at[1]).wait()
        self.row[self.z] = jnp.sum(self.piece[...].astype(F32), axis=0).astype(BF16)
        for k in range(1, RING):
            _, peer = self.along_z(k)
            send_to(peer, self.row.at[self.z], self.row.at[self.z], self.sems.at[2]).start()

    def start_fourth(self):
        rest = pl.ds(0, RING - 1)
        send_to(self.along_z(1)[1], self.row.at[rest], self.row.at[rest], self.sems.at[2]).wait()
        for k in range(1, RING):
            _, peer = self.along_xc(k)
            send_to(peer, self.row, self.out.at[self.xc], self.sems.at[3]).start()
        self.out[self.xc] = self.row[...]

    def finish(self):
        rest = pl.ds(0, RING - 1)
        send_to(self.along_xc(1)[1], self.tiles.at[rest], self.out.at[rest], self.sems.at[3]).wait()


def main_kernel(
    query_hbm, key_hbm, value_hbm, grad_hbm, rand_hbm, pos_hbm,
    attended, grad_query, own, edge_back, tiles_back, slots_back, table, hot_out,
    rand, rand_smem, pos, table_smem, given_vmem, given_smem, query, key, value, grad, stacked, slots_out, slots, edge, tiles_in, part, middle, piece, row, tiles,
    near_s, near_g, glob_s, glob_g, near_p, near_d, glob_d, glob_p, far_d, row_max, row_sum, picked,
    edge_grads, back_in, back_part, back_middle, back_piece, back_row, back_out,
    local_sems, edge_sems, tile_sems, slot_sems, edge_back_sems, tile_back_sems, slot_back_sems,
):
    me = lax.axis_index("seq")
    right, left = lax.rem(me + 1, SEQ), lax.rem(me + SEQ - 1, SEQ)
    barrier = pltpu.get_barrier_semaphore()
    loads = [
        pltpu.make_async_copy(src, dst, local_sems.at[i])
        for i, (src, dst) in enumerate(
            (
                (rand_hbm, rand),
                (rand_hbm, rand_smem),
                (pos_hbm, pos),
                (key_hbm, key),
                (value_hbm, value),
                (query_hbm, query),
                (grad_hbm, grad),
            )
        )
    ]
    for copy in loads:
        copy.start()

    @pl.loop(1, SEQ)
    def _(k):
        pl.semaphore_signal(barrier, inc=1, device_id={"seq": lax.rem(me + k, SEQ)}, device_id_type=MESH)

    for copy in loads[:5]:
        copy.wait()

    asked = jnp.zeros((HEADS, SEQ * BLOCKS), jnp.int32)
    for p in range(PICKS):
        names = rand[p]
        code = (names & (BLOCKS - 1)) * HEADS + lax.broadcasted_iota(jnp.int32, names.shape, 0) + 1
        asked = jnp.maximum(asked, jnp.where(names >> 2 == me, code, 0))
    asked = jnp.max(asked, axis=0, keepdims=True)
    line = lax.broadcasted_iota(jnp.int32, (8, SEQ * BLOCKS), 0)
    table[...] = jnp.where(line == MINE, me, asked)
    holder = lambda h, j, p: rand_smem[p, h, me * BLOCKS + j] >> 2
    lane = lax.broadcasted_iota(jnp.int32, (8, DIM), 1)
    found = jnp.full((8, DIM), NPICK, jnp.int32)
    for h in range(HEADS):
        for j in range(BLOCKS):
            for p in range(PICKS):
                found = jnp.where(lane == holder(h, j, p), (h * BLOCKS + j) * PICKS + p, found)
    given_vmem[...] = found
    copies = [
        pltpu.make_async_copy(table, table_smem, local_sems.at[7]),
        pltpu.make_async_copy(given_vmem, given_smem, local_sems.at[8]),
    ]
    for copy in copies:
        copy.start()
    given = lambda k: given_smem[0, k]
    want = lambda k: jnp.maximum(named_by(table_smem, k) - 1, 0)

    for j in range(BLOCKS):
        for h in range(HEADS):
            rows, cols = pl.ds(j * BLOCK, BLOCK), pl.ds(h * DIM, DIM)
            stacked[j * HEADS + h, UPPER] = key[rows, cols]
            stacked[j * HEADS + h, LOWER] = value[rows, cols]
    hot = (lax.broadcasted_iota(jnp.int32, (TOK, GLOB), 0) == pos[...] - me * TOK).astype(F32).astype(BF16)
    hot_out[...] = hot
    for c, ref in enumerate((key, value)):
        owned = dot_tn(hot, ref[...]).astype(BF16)
        for g in range(GROUPS):
            for h in range(HEADS):
                tiles_in[g, c * HEADS + h] = owned[g * TILE : (g + 1) * TILE, h * DIM : (h + 1) * DIM]

    for copy in copies:
        copy.wait()

    @pl.loop(0, SEQ)
    def _(k):
        slots_out[k] = stacked[want(k)]

    slots[me] = slots_out[me]

    def send_slots(chunk):
        @pl.loop(CHUNKS[chunk], CHUNKS[chunk + 1])
        def _(k):
            peer = lax.rem(me + k, SEQ)
            send_to(peer, slots_out.at[peer], slots.at[me], slot_sems).start()

    pl.semaphore_wait(barrier, SEQ - 1)
    last, first = pl.ds(TOK - BLOCK, BLOCK), pl.ds(0, BLOCK)
    edges = [
        send_to(left, key.at[first], edge.at[1, UPPER], edge_sems.at[0]),
        send_to(left, value.at[first], edge.at[1, LOWER], edge_sems.at[1]),
        send_to(right, key.at[last], edge.at[0, UPPER], edge_sems.at[2]),
        send_to(right, value.at[last], edge.at[0, LOWER], edge_sems.at[3]),
    ]
    shared = Tiles(me, tiles_in, part, middle, piece, row, tiles, tile_sems)
    shared.start_first()
    for copy in edges:
        copy.start()
    send_slots(0)
    shared.start_second()
    send_slots(1)
    shared.start_third()
    send_slots(2)
    shared.start_fourth()
    send_slots(3)

    loads[5].wait()
    loads[6].wait()
    for copy in edges:
        copy.wait()
    query_block = lax.broadcasted_iota(jnp.int32, (TOK, WIDE), 0) // BLOCK
    key_block = lax.broadcasted_iota(jnp.int32, (TOK, WIDE), 1) // BLOCK
    low = jnp.where(me == 0, 1, 0)
    high = jnp.where(me == SEQ - 1, BLOCKS, BLOCKS + 1)
    offset = key_block - query_block
    band = (offset >= 0) & (offset <= 2) & (key_block >= low) & (key_block <= high)

    def near_keys(cols):
        return jnp.concatenate([edge[0, UPPER, cols], key[:, cols], edge[1, UPPER, cols]], axis=0)

    def near_values(cols):
        return jnp.concatenate([edge[0, LOWER, cols], value[:, cols], edge[1, LOWER, cols]], axis=0)

    def glob_keys(h):
        return jnp.concatenate([tiles[g, h] for g in range(GROUPS)], axis=0)

    def glob_values(h):
        return jnp.concatenate([tiles[g, HEADS + h] for g in range(GROUPS)], axis=0)

    for h in range(HEADS):
        cols = pl.ds(h * DIM, DIM)
        near_s[h] = jnp.where(band, dot_nt(query[:, cols], near_keys(cols)) * SCALE, -1e30)
        near_g[h] = dot_nt(grad[:, cols], near_values(cols))
    shared.finish()
    for h in range(HEADS):
        cols = pl.ds(h * DIM, DIM)
        near, glob = near_s[h], dot_nt(query[:, cols], glob_keys(h)) * SCALE
        top = jnp.maximum(jnp.max(near, axis=1, keepdims=True), jnp.max(glob, axis=1, keepdims=True))
        near, glob = jnp.exp(near - top), jnp.exp(glob - top)
        near_s[h], glob_s[h] = near, glob
        row_max[h] = jnp.broadcast_to(top, (TOK, DIM))
        row_sum[h] = jnp.broadcast_to(
            jnp.sum(near, axis=1, keepdims=True) + jnp.sum(glob, axis=1, keepdims=True), (TOK, DIM)
        )
        glob_g[h] = dot_nt(grad[:, cols], glob_values(h))
    rest = pl.ds(0, SEQ - 1)
    send_to(right, slots_out.at[rest], slots.at[rest], slot_sems).wait()

    block_rows = [slice(j * BLOCK, (j + 1) * BLOCK) for j in range(BLOCKS)]
    picked[NPICK] = jnp.zeros((2 * BLOCK, DIM), BF16)

    def far_keys(h, j):
        return jnp.concatenate([slots[holder(h, j, p), UPPER] for p in range(PICKS)], axis=0)

    for h in range(HEADS):
        cols = pl.ds(h * DIM, DIM)
        q, g = query[:, cols], grad[:, cols]
        keys = [far_keys(h, j) for j in range(BLOCKS)]
        values = [jnp.concatenate([slots[holder(h, j, p), LOWER] for p in range(PICKS)], axis=0) for j in range(BLOCKS)]
        far = jnp.concatenate([dot_nt(q[block_rows[j]], keys[j]) for j in range(BLOCKS)], axis=0) * SCALE
        old_max, old_sum = row_max[h, :, :1], row_sum[h, :, :1]
        new_max = jnp.maximum(old_max, jnp.max(far, axis=1, keepdims=True))
        far = jnp.exp(far - new_max)
        shrink = jnp.exp(old_max - new_max)
        inverse = 1.0 / (old_sum * shrink + jnp.sum(far, axis=1, keepdims=True))
        near, far, glob = near_s[h] * (shrink * inverse), far * inverse, glob_s[h] * (shrink * inverse)
        near_b, far_b, glob_b = near.astype(BF16), far.astype(BF16), glob.astype(BF16)
        mixed = dot_nn(near_b, near_values(cols)) + dot_nn(glob_b, glob_values(h))
        mixed += jnp.concatenate([dot_nn(far_b[block_rows[j]], values[j]) for j in range(BLOCKS)], axis=0)
        attended[:, cols] = mixed.astype(BF16)
        delta = jnp.sum(g.astype(F32) * mixed, axis=1, keepdims=True)
        far_g = jnp.concatenate([dot_nt(g[block_rows[j]], values[j]) for j in range(BLOCKS)], axis=0)
        far_change = (far * (far_g - delta)).astype(BF16)
        far_d[h] = far_change
        for j in range(BLOCKS):
            far_key = (dot_tn(far_change[block_rows[j]], q[block_rows[j]]) * SCALE).astype(BF16)
            far_value = dot_tn(far_b[block_rows[j]], g[block_rows[j]]).astype(BF16)
            for p in range(PICKS):
                at = (h * BLOCKS + j) * PICKS + p
                picked[at, UPPER] = far_key[p * BLOCK : (p + 1) * BLOCK]
                picked[at, LOWER] = far_value[p * BLOCK : (p + 1) * BLOCK]
        near_p[h] = near_b
        glob_p[h] = glob_b
        near_d[h] = (near * (near_g[h] - delta)).astype(BF16)
        glob_d[h] = (glob * (glob_g[h] - delta)).astype(BF16)

    def return_slots(begin, end):
        @pl.loop(begin, end)
        def _(k):
            peer = lax.rem(me + k, SEQ)
            slots_out[peer] = picked[given(peer)]
            send_to(peer, slots_out.at[peer], slots_back.at[me], slot_back_sems).start()

    return_slots(CHUNKS[0], EARLY)
    for h in range(HEADS):
        cols = pl.ds(h * DIM, DIM)
        glob_key = (dot_tn(glob_d[h], query[:, cols]) * SCALE).astype(BF16)
        glob_value = dot_tn(glob_p[h], grad[:, cols]).astype(BF16)
        for g in range(GROUPS):
            back_in[g, h] = glob_key[g * TILE : (g + 1) * TILE]
            back_in[g, HEADS + h] = glob_value[g * TILE : (g + 1) * TILE]
    summed = Tiles(me, back_in, back_part, back_middle, back_piece, back_row, back_out, tile_back_sems)
    summed.start_first()
    return_slots(EARLY, CHUNKS[1])
    slots_back[me] = picked[given(me)]
    for h in range(HEADS):
        cols = pl.ds(h * DIM, DIM)
        q, g = query[:, cols], grad[:, cols]
        near_key = dot_tn(near_d[h], q) * SCALE
        near_value = dot_tn(near_p[h], g)
        for j in range(BLOCKS):
            own[j * HEADS + h, UPPER] = near_key[(j + 1) * BLOCK : (j + 2) * BLOCK]
            own[j * HEADS + h, LOWER] = near_value[(j + 1) * BLOCK : (j + 2) * BLOCK]
        edge_grads[0, UPPER, cols] = near_key[:BLOCK].astype(BF16)
        edge_grads[0, LOWER, cols] = near_value[:BLOCK].astype(BF16)
        edge_grads[1, UPPER, cols] = near_key[BLOCK + TOK :].astype(BF16)
        edge_grads[1, LOWER, cols] = near_value[BLOCK + TOK :].astype(BF16)
    edges = [
        send_to(left, edge_grads.at[0], edge_back.at[1], edge_back_sems.at[0]),
        send_to(right, edge_grads.at[1], edge_back.at[0], edge_back_sems.at[1]),
    ]
    for copy in edges:
        copy.start()
    summed.start_second()
    return_slots(CHUNKS[1], CHUNKS[2])
    summed.start_third()
    return_slots(CHUNKS[2], CHUNKS[3])
    summed.start_fourth()
    return_slots(CHUNKS[3], CHUNKS[4])
    for h in range(HEADS):
        cols = pl.ds(h * DIM, DIM)
        change = dot_nn(near_d[h], near_keys(cols)) + dot_nn(glob_d[h], glob_keys(h))
        change += jnp.concatenate([dot_nn(far_d[h, block_rows[j]], far_keys(h, j)) for j in range(BLOCKS)], axis=0)
        grad_query[:, cols] = (change * SCALE).astype(BF16)
    summed.finish()
    tiles_back[...] = back_out[...]
    for copy in edges:
        copy.wait()
    send_to(right, slots_out.at[rest], slots_back.at[rest], slot_back_sems).wait()


def collect_kernel(
    table, hot, attended_in, query_in, own, edge, tiles, slots,
    attended, grad_query, grad_key, grad_value, total, sems,
):
    me = table[MINE, 0]
    passed = [
        pltpu.make_async_copy(attended_in, attended, sems.at[0]),
        pltpu.make_async_copy(query_in, grad_query, sems.at[1]),
    ]
    for copy in passed:
        copy.start()
    total[...] = own[...]

    @pl.loop(0, SEQ)
    def _(k):
        target = named_by(table, k)

        @pl.when(target > 0)
        def _():
            total[target - 1] += slots[k].astype(F32)

    from_left = jnp.where(me == 0, 0.0, 1.0)
    from_right = jnp.where(me == SEQ - 1, 0.0, 1.0)
    for h in range(HEADS):
        cols = pl.ds(h * DIM, DIM)
        for c, out in enumerate((grad_key, grad_value)):
            part = pl.ds(c * BLOCK, BLOCK)
            glob = jnp.concatenate([tiles[g, c * HEADS + h] for g in range(GROUPS)], axis=0)
            placed = dot_nn(hot[...], glob)
            for j in range(BLOCKS):
                whole = total[j * HEADS + h, part] + placed[j * BLOCK : (j + 1) * BLOCK]
                if j == 0:
                    whole += edge[0, part, cols].astype(F32) * from_left
                if j == BLOCKS - 1:
                    whole += edge[1, part, cols].astype(F32) * from_right
                out[pl.ds(j * BLOCK, BLOCK), cols] = whole.astype(BF16)
    for copy in passed:
        copy.wait()


def body(query_rows, key_rows, value_rows, grad_out, rand_blocks, global_pos):
    arrays = [a.reshape(TOK, COLS) for a in (query_rows, key_rows, value_rows, grad_out)]
    names = rand_blocks.transpose(0, 3, 1, 2).reshape(PICKS, HEADS, SEQ * BLOCKS)
    pos = global_pos[None, :]
    operands = [pltpu.with_memory_space_constraint(a, pltpu.HBM) for a in (*arrays, names, pos)]
    shape = jax.ShapeDtypeStruct
    slot_shape, edge_shape = (SEQ, 2 * BLOCK, DIM), (2, 2 * BLOCK, COLS)
    grid_shape, row_shape = (RING, RING, TILE, DIM), (RING, TILE, DIM)
    own_shape, narrow = shape((BLOCKS * HEADS, 2 * BLOCK, DIM), F32), shape((TOK, COLS), BF16)
    bf16 = lambda dims: pltpu.VMEM(dims, BF16)
    f32 = lambda dims: pltpu.VMEM(dims, F32)
    dma = pltpu.SemaphoreType.DMA
    tile_scratch = [bf16(grid_shape), bf16(grid_shape), bf16(row_shape), bf16(row_shape), bf16(row_shape), bf16(grid_shape)]
    attended, grad_query, own, edge, tiles, slots, table, hot = pl.pallas_call(
        main_kernel,
        out_shape=[
            *[narrow, narrow, own_shape],
            *[shape(dims, BF16) for dims in (edge_shape, grid_shape, slot_shape)],
            shape((8, SEQ * BLOCKS), jnp.int32),
            shape((TOK, GLOB), BF16),
        ],
        in_specs=[ANY] * 6,
        out_specs=[VMEM] * 8,
        scratch_shapes=[
            pltpu.VMEM((PICKS, HEADS, SEQ * BLOCKS), jnp.int32),
            pltpu.SMEM((PICKS, HEADS, SEQ * BLOCKS), jnp.int32),
            pltpu.VMEM((1, GLOB), jnp.int32),
            pltpu.SMEM((8, SEQ * BLOCKS), jnp.int32),
            pltpu.VMEM((8, DIM), jnp.int32),
            pltpu.SMEM((8, DIM), jnp.int32),
            *[bf16((TOK, COLS))] * 4,
            bf16((BLOCKS * HEADS, 2 * BLOCK, DIM)),
            bf16(slot_shape),
            bf16(slot_shape),
            bf16(edge_shape),
            *tile_scratch,
            f32((HEADS, TOK, WIDE)),
            f32((HEADS, TOK, WIDE)),
            f32((HEADS, TOK, GLOB)),
            f32((HEADS, TOK, GLOB)),
            bf16((HEADS, TOK, WIDE)),
            bf16((HEADS, TOK, WIDE)),
            bf16((HEADS, TOK, GLOB)),
            bf16((HEADS, TOK, GLOB)),
            bf16((HEADS, TOK, FAR)),
            f32((HEADS, TOK, DIM)),
            f32((HEADS, TOK, DIM)),
            bf16((NPICK + 1, 2 * BLOCK, DIM)),
            bf16(edge_shape),
            *tile_scratch,
            dma((9,)),
            dma((4, 2)),
            dma((4, 2)),
            dma((2,)),
            dma((2, 2)),
            dma((4, 2)),
            dma((2,)),
        ],
        compiler_params=pltpu.CompilerParams(
            collective_id=0, has_side_effects=True, vmem_limit_bytes=48 << 20
        ),
        name="attend",
    )(*operands)
    results = pl.pallas_call(
        collect_kernel,
        out_shape=[narrow] * 4,
        in_specs=[SMEM] + [VMEM] * 7,
        out_specs=[ANY, ANY, VMEM, VMEM],
        scratch_shapes=[f32((BLOCKS * HEADS, 2 * BLOCK, DIM)), dma((2,))],
        compiler_params=pltpu.CompilerParams(vmem_limit_bytes=32 << 20),
        name="collect",
    )(table, hot, attended, grad_query, own, edge, tiles, slots)
    return tuple(a.reshape(1, TOK, COLS) for a in results)


def solution(mesh):
    rows = P(None, "seq", "head")
    return jax.shard_map(
        body,
        mesh=mesh,
        in_specs=(rows, rows, rows, rows, P(None, "head", None, None), P()),
        out_specs=(rows, rows, rows, rows),
        check_vma=False,
    )
```
